32 devices in a mesh: parts: 2 (over x), row: 16 (over z, y, core).
Axes of the slice: x: 2, y: 2, z: 4, core: 2. Of those that a mesh axis runs over, the one named last changes fastest.
Arguments:
- tile_values: bfloat16 [2048, 128, 128], P(('parts', 'row')), parts along dimension 0, may hold values from -0.09375 to 0.09375
- tile_row: int32 [2048], P(('parts', 'row')), parts along dimension 0, may hold values from 0 to 1
- tile_col: int32 [2048], P(('parts', 'row')), parts along dimension 0, may hold values from 0 to 15
- primal_start: float32 [4096, 128], P(('parts', 'row')), parts along dimension 0, may hold values from 0 to 1
- objective: float32 [4096, 128], P(('parts', 'row')), parts along dimension 0, may hold values from -3 to 3
- upper_bound: float32 [4096], P(('parts', 'row')), parts along dimension 0, may hold values from 0.3 to 3
- dual_start: float32 [8192, 128], P(('parts', 'row')), parts along dimension 0, may hold values from 0 to 1
- row_bound: float32 [8192, 128], P(('parts', 'row')), parts along dimension 0, may hold values from -6 to 6
Outputs:
- primal: float32 [4096, 128], P(('parts', 'row')), parts along dimension 0
- dual: float32 [8192, 128], P(('parts', 'row')), parts along dimension 0
The draws below stay inside these ranges and needn't reach their ends.
There are 2 independent parts, one for each index of `parts`. The reference program is written for one: setup_inputs(seed, part) draws one part's arguments, and reference() takes and returns one part's arrays. A program takes and returns all parts, laid end to end along the dimension named above; each array names one. Nothing has to cross between parts.
All inputs are finite; a program needn't handle non-finite values.
Results may differ from the reference program's by a relative error of at most 0.0023.
Values may be sent and summed in bfloat16 or wider, within the bound.
A program may use at most 64 MiB of HBM per device.

```python
import math
import jax
import jax.numpy as jnp
from jax import lax

S = 128
TB = 128
TILES_DEV = 64
RB_DEV = 2
ITERS = 3
NTILES = 1024
NRB = 32
NCB = 16
NROWS = 4096
NCOLS = 2048
N_ROW = 16


def plant(array, rng, low, high):
    place = [jax.random.randint(jax.random.fold_in(rng, axis), (), 0, length) for axis, length in enumerate(array.shape)]
    widest = array.shape.index(max(array.shape))
    next_to = place[:widest] + [(place[widest] + 1) % array.shape[widest]] + place[widest + 1:]
    return array.at[tuple(place)].set(low).at[tuple(next_to)].set(high)


def block_levels(stream_key, extent, cuts, low, high):
    def one(axis_at, parts):
        heights = jax.random.uniform(jax.random.fold_in(jax.random.fold_in(stream_key, 6), axis_at), (parts,), jnp.float32, low / len(cuts), high / len(cuts))
        return jnp.repeat(jnp.exp(heights), extent[axis_at] // parts).reshape((-1,) + (1,) * (len(extent) - axis_at - 1))

    gain = one(*cuts[0])
    for cut in cuts[1:]:
        gain = gain * one(*cut)
    return gain


def gaussian(stream_key, dims, width, limit, cuts=(), held_as=jnp.bfloat16):
    drawn = jax.random.normal(stream_key, dims, jnp.float32) * width
    if len(cuts) > 0:
        drawn = block_levels(stream_key, dims, cuts, -0.22, 0.18) * drawn
    return jnp.clip(drawn, min=-limit, max=limit).astype(held_as)


def setup_inputs(seed: int = 0, part: int = 0) -> dict:
    streams_of = jax.random.split(jax.random.key(seed), 9)
    part_keys = jax.random.split(jax.random.fold_in(streams_of[8], part), 9)
    tile_values = gaussian(part_keys[0], (NTILES, TB, TB), (TB * TILES_DEV // RB_DEV) ** -0.5, 0.09375, ((0, 16),))
    tile_row = plant(jax.random.randint(part_keys[1], (NTILES,), 0, RB_DEV), jax.random.fold_in(part_keys[1], 1), 0, RB_DEV - 1).astype(jnp.int32)
    tile_col = plant(jax.random.randint(part_keys[2], (NTILES,), 0, NCB), jax.random.fold_in(part_keys[2], 1), 0, NCB - 1).astype(jnp.int32)
    primal_start = jnp.clip(1.0 * jax.random.uniform(part_keys[3], (NCOLS, S), jnp.float32) ** block_levels(part_keys[3], (NCOLS, S), ((0, 16),), -0.2, 0.2), 0.0, 1.0)
    objective = gaussian(part_keys[4], (NCOLS, S), 0.5, 3.0, ((0, 16),), jnp.float32)
    upper_bound = jnp.clip(jnp.exp(math.log(3.0) - 2.3025851 * jax.random.uniform(part_keys[5], (NCOLS,), jnp.float32) ** block_levels(part_keys[5], (NCOLS,), ((0, 16),), -0.2, 0.2)), 0.3, 3.0)
    dual_start = jnp.clip(1.0 * jax.random.uniform(part_keys[6], (NROWS, S), jnp.float32) ** block_levels(part_keys[6], (NROWS, S), ((0, 16),), -0.2, 0.2), 0.0, 1.0)
    row_bound = gaussian(part_keys[7], (NROWS, S), 1.0, 6.0, ((0, 16),), jnp.float32)
    return {"tile_values": tile_values, "tile_row": tile_row, "tile_col": tile_col, "primal_start": primal_start, "objective": objective, "upper_bound": upper_bound, "dual_start": dual_start, "row_bound": row_bound}


def reference(tile_values, tile_row, tile_col, primal_start, objective, upper_bound, dual_start, row_bound):
    stacked = tile_values.reshape(N_ROW, TILES_DEV, TB, TB)
    rows_local = tile_row.reshape(N_ROW, TILES_DEV).astype(jnp.int32)
    offsets = (jnp.arange(N_ROW, dtype=jnp.int32) * RB_DEV)[:, None]
    rows_global = (rows_local + offsets).astype(jnp.int32)
    cols_here = tile_col.reshape(N_ROW, TILES_DEV).astype(jnp.int32)
    primal = primal_start
    dual = dual_start
    for iteration in range(ITERS):
        dual_blocks = dual.astype(jnp.bfloat16).reshape(NRB, TB, S)

        def add_device(total, inputs):
            values, rows_now, cols_now = inputs
            picked = dual_blocks[rows_now].astype(jnp.float32)
            partial_value = jnp.einsum('tij,tis->tjs', values.astype(jnp.float32), picked)
            return total + jax.ops.segment_sum(partial_value, cols_now, num_segments=NCB), None

        column_sum, _ = lax.scan(add_device, jnp.zeros((NCB, TB, S), jnp.float32), (stacked, rows_global, cols_here))
        column_sum = column_sum.reshape(NCOLS, S)
        updated = jnp.clip(primal - 0.4 * (objective - column_sum), 0.0, upper_bound[:, None])
        extrapolated = (2.0 * updated - primal).astype(jnp.bfloat16).reshape(NCB, TB, S)

        def image_device(carry, inputs):
            values, rows_now, cols_now = inputs
            chosen = extrapolated[cols_now].astype(jnp.float32)
            products = jnp.einsum('tij,tjs->tis', values.astype(jnp.float32), chosen)
            return carry, jax.ops.segment_sum(products, rows_now, num_segments=RB_DEV)

        _, images = lax.scan(image_device, jnp.zeros((), jnp.float32), (stacked, rows_local, cols_here))
        row_image = images.reshape(NROWS, S)
        dual = jnp.maximum(dual + 0.4 * (row_bound - row_image), 0.0)
        primal = updated
    return primal, dual
```

```python
import functools

import jax
import jax.numpy as jnp
from jax import lax
from jax.experimental import pallas as pl
from jax.experimental.pallas import tpu as pltpu
from jax.sharding import PartitionSpec as P

ITERS = 3
CHAINS = 2
STEP = 0.4
F32 = jnp.float32
BF16 = jnp.bfloat16


def dense_kernel(places, tiles, high, low, total):
    total[...] = jnp.zeros_like(total)

    @pl.loop(0, tiles.shape[0], unroll=8)
    def _(t):
        total[places[t]] += tiles[t].astype(F32)

    @pl.loop(0, total.shape[0], unroll=4)
    def _(b):
        value = total[b]
        rounded = value.astype(BF16)
        high[b] = rounded
        low[b] = (value - rounded.astype(F32)).astype(BF16)


def dense(tile_values, tile_row, tile_col, blocks, row_blocks):
    tiles, size, _ = tile_values.shape
    shape = jax.ShapeDtypeStruct((blocks * row_blocks, size, size), BF16)
    smem = pl.BlockSpec(memory_space=pltpu.SMEM)
    vmem = pl.BlockSpec(memory_space=pltpu.VMEM)
    room = size * size * (8 * blocks * row_blocks + 2 * tiles)
    return pl.pallas_call(
        dense_kernel,
        out_shape=(shape, shape),
        in_specs=[smem, vmem],
        out_specs=(vmem, vmem),
        scratch_shapes=[pltpu.VMEM((blocks * row_blocks, size, size), F32)],
        compiler_params=pltpu.CompilerParams(vmem_limit_bytes=room + (4 << 20)),
    )(tile_col * row_blocks + tile_row, tile_values)


def iterate_kernel(
    n, chains, high, low, primal_start, objective, upper, dual_start, row_bound,
    primal_out, dual_out,
    far_high, far_low, flipped, bounds, packed, state, dual, bound,
    part_own, part_send, part_recv, own, send1, recv1, half, send2, recv2, spread,
    primal_end, dual_end,
    sp, rp, sa, ra, sd, rd, si, ri, s1, r1, s2, r2, sx, rx, se, re,
):
    me = lax.axis_index("row")
    core = lax.rem(me, 2)
    chip = me // 2
    group = n // 4
    side = chip // group
    seat = lax.rem(chip, group)
    partner = me + 1 - 2 * core
    mirror = lax.rem(chip + group, 2 * group) * 2
    size = primal_start.shape[0]
    rows = dual_start.shape[0]
    mine = primal_start.shape[1] // 2
    part = mine // chains
    slot = 2 * side

    def seat_at(d):
        return lax.bitwise_xor(seat, d)

    def peer(d):
        return (side * group + seat_at(d)) * 2 + core

    def send(src, dst, send_sem, recv_sem, device):
        return pltpu.make_async_remote_copy(
            src_ref=src, dst_ref=dst, send_sem=send_sem, recv_sem=recv_sem,
            device_id={"row": device}, device_id_type=pl.DeviceIdType.MESH,
        )

    def whole(h):
        return pl.ds(h * mine, mine)

    def chain(c):
        return pl.ds(c * part, part)

    def place(c):
        return pl.ds(core * mine + c * part, part)

    def first_partial(d):
        return send(part_send.at[d], part_recv.at[d], sp.at[d], rp.at[d], partner)

    def matrix(k):
        src, dst = ((high, far_high), (low, far_low))[k]
        return send(src, dst, sa.at[k], ra.at[k], partner)

    def rows_over(k):
        src, dst = ((flipped, dual), (bounds, bound))[k]
        return send(src.at[whole(1 - core)], dst.at[1], sd.at[k], rd.at[k], partner)

    def start_state(k):
        source = packed.at[core if k == 1 else 1 - core]
        device = (partner, mirror + core, mirror + 1 - core)[k]
        return send(source, state.at[slot + core], si.at[k], ri.at[k], device)

    def reduce(c, d):
        return send(send1.at[c, d], recv1.at[c, d], s1.at[c, d], r1.at[c, d], peer(d))

    def cross(c, step):
        turn = lax.rem(step, 2)
        return send(
            send2.at[c, turn], recv2.at[c, turn], s2.at[c, turn], r2.at[c, turn], mirror + core
        )

    def gather(c, d):
        return send(spread.at[c, 0], spread.at[c, d], sx.at[c, d], rx.at[c, d], peer(d))

    def primal_back(c):
        return send(
            state.at[slot + 1 - core, chain(c)], primal_end.at[place(c)],
            se.at[0, c], re.at[0, c], partner,
        )

    def dual_back(c):
        return send(
            dual.at[1, chain(c)], dual_end.at[place(c)], se.at[1, c], re.at[1, c], partner
        )

    far_first = list(range(group - 1, 0, -1))
    near_first = list(range(1, group))

    def owned(d):
        q = seat_at(d)
        return [2 * q, 2 * q + 1, 2 * (q + group), 2 * (q + group) + 1]

    def dot(left, right, axis):
        return lax.dot_general(
            left, right, (((1,), (axis,)), ((), ())), preferred_element_type=F32
        )

    def side_by_side(ref, blocks):
        return jnp.concatenate([ref[b] for b in blocks], axis=1)

    def columns(left, blocks, pairs):
        total = None
        for refs in pairs:
            right = jnp.concatenate([side_by_side(ref, blocks) for ref in refs], axis=0)
            value = dot(left, right, 0)
            total = value if total is None else total + value
        return total

    near = ((high,), (low,))
    both = ((high, far_high), (low, far_low))

    def start():
        left = jnp.concatenate([flipped[whole(core), :], flipped[whole(1 - core), :]], axis=0)
        left = left.astype(BF16)
        for d in far_first + [0]:
            blocks = owned(d)
            for i in range(0, 4, 2):
                value = columns(left, blocks[i : i + 2], near)
                for k in range(2):
                    piece = value[:, k * size : (k + 1) * size]
                    part_own[d, i + k] = piece[:mine]
                    part_send[d, i + k] = piece[mine:].astype(BF16)

    def finish_start():
        for d in far_first + [0]:
            first_partial(d).wait_recv()
            for c in range(chains):
                value = part_own[d, :, chain(c)] + part_recv[d, :, chain(c)].astype(F32)
                if d:
                    send1[c, d] = value.astype(BF16)
                    reduce(c, d).start()
                else:
                    own[c] = value

    def partials(c):
        left = jnp.concatenate([dual[0, chain(c), :], dual[1, chain(c), :]], axis=1)
        left = left.astype(BF16)
        for d in far_first + [0]:
            blocks = owned(d)
            for i in range(0, 4, 2):
                value = columns(left, blocks[i : i + 2], both)
                for k in range(2):
                    piece = value[:, k * size : (k + 1) * size]
                    if d:
                        send1[c, d, i + k] = piece.astype(BF16)
                    else:
                        own[c, i + k] = piece
            if d:
                reduce(c, d).start()

    def merge(c, step):
        total = own[c]
        for d in near_first:
            reduce(c, d).wait_recv()
            total += recv1[c, d].astype(F32)
        half[c] = total
        send2[c, lax.rem(step, 2)] = total.astype(BF16)
        cross(c, step).start()

    def update(c, step):
        cross(c, step).wait_recv()
        total = half[c] + recv2[c, lax.rem(step, 2)].astype(F32)
        before = state[:, chain(c), :]
        cost = state[:, pl.ds(mine + c * part, part), :]
        upper_here = state[:, pl.ds(2 * mine, 1), :]
        updated = jnp.clip(before - STEP * (cost - total), 0.0, upper_here)
        spread[c, 0] = (2.0 * updated - before).astype(BF16)
        for d in far_first:
            gather(c, d).start()
        state[:, chain(c), :] = updated
        for d in near_first:
            reduce(c, d).wait_send()
        cross(c, step).wait_send()

    def image(c):
        total = None
        for d in [0] + near_first:
            if d:
                gather(c, d).wait_recv()
            blocks = owned(d)
            left = jnp.concatenate([spread[c, d, i] for i in range(4)], axis=1)
            for refs in both:
                right = jnp.concatenate([side_by_side(ref, blocks) for ref in refs], axis=0)
                value = dot(left, right, 1)
                total = value if total is None else total + value
        for k in range(2):
            dual[k, chain(c), :] = jnp.maximum(
                dual[k, chain(c), :]
                + STEP * (bound[k, chain(c), :] - total[:, k * rows : (k + 1) * rows]),
                0.0,
            )
        for d in near_first:
            gather(c, d).wait_send()

    barrier = pltpu.get_barrier_semaphore()
    others = [partner, mirror + core, mirror + 1 - core] + [peer(d) for d in near_first]
    for other in others:
        pl.semaphore_signal(
            barrier, inc=1, device_id={"row": other}, device_id_type=pl.DeviceIdType.MESH
        )
    flipped[...] = dual_start[...].T
    for source, offset in ((primal_start, 0), (objective, mine)):
        value = source[...].T
        for h in range(2):
            packed[h, pl.ds(offset, mine), :] = value[h * mine : (h + 1) * mine]
    for h in range(2):
        packed[h, pl.ds(2 * mine, 8), :] = jnp.broadcast_to(upper[...], (8, size))
    bounds[...] = row_bound[...].T
    start()
    pl.semaphore_wait(barrier, len(others))
    for d in far_first + [0]:
        first_partial(d).start()
    for k in (1, 2, 0):
        start_state(k).start()
    for k in range(2):
        rows_over(k).start()
    for k in range(2):
        matrix(k).start()
    state[slot + core] = packed[core]
    dual[0] = flipped[whole(core), :]
    bound[0] = bounds[whole(core), :]
    finish_start()
    for c in range(chains):
        merge(c, 0)
    for k in range(3):
        start_state(k).wait()
    for k in range(2):
        rows_over(k).wait()
        matrix(k).wait()
    for d in range(group):
        first_partial(d).wait_send()

    def iteration(step, carry):
        more = step < ITERS - 1
        for c in range(chains):
            update(c, step)

            @pl.when(jnp.logical_not(more))
            def _():
                primal_back(c).start()

        for c in range(chains):
            image(c)
            pl.when(more)(functools.partial(partials, c))

            @pl.when(jnp.logical_not(more))
            def _():
                dual_back(c).start()

        @pl.when(more)
        def _():
            for c in range(chains):
                merge(c, step + 1)

        return carry

    lax.fori_loop(0, ITERS, iteration, 0)
    for c in range(chains):
        primal_end[place(c), :] = state[slot + core, chain(c), :]
        dual_end[place(c), :] = dual[0, chain(c), :]
    for c in range(chains):
        primal_back(c).wait()
    primal_out[...] = primal_end[...].T
    for c in range(chains):
        dual_back(c).wait()
    dual_out[...] = dual_end[...].T


def body(
    tile_values, tile_row, tile_col, primal_start, objective, upper_bound, dual_start, row_bound
):
    n = lax.axis_size("row")
    size = tile_values.shape[1]
    count = primal_start.shape[1]
    blocks = n * primal_start.shape[0] // size
    group = n // 4
    assert blocks == n and n % 4 == 0 and group & (group - 1) == 0
    rows = dual_start.shape[0]
    row_blocks = rows // size
    high, low = dense(tile_values, tile_row, tile_col, blocks, row_blocks)
    chains = CHAINS
    mine = count // 2
    part = mine // chains
    vmem = pl.BlockSpec(memory_space=pltpu.VMEM)
    dma = pltpu.SemaphoreType.DMA
    matrix = pltpu.VMEM((blocks, rows, size), BF16)
    pieces = pltpu.VMEM((chains, group, 4, part, size), BF16)
    sums = pltpu.VMEM((chains, 4, part, size), F32)
    turns = pltpu.VMEM((chains, 2, 4, part, size), BF16)
    room = 4 * blocks * rows * size + 4 * blocks * mine * size * 8 + (8 << 20)
    return pl.pallas_call(
        functools.partial(iterate_kernel, n, chains),
        out_shape=(
            jax.ShapeDtypeStruct(primal_start.shape, F32),
            jax.ShapeDtypeStruct(dual_start.shape, F32),
        ),
        in_specs=[vmem] * 7,
        out_specs=(vmem, vmem),
        scratch_shapes=[
            matrix, matrix,
            pltpu.VMEM((count, rows), F32), pltpu.VMEM((count, rows), F32),
            pltpu.VMEM((2, count + 8, size), F32), pltpu.VMEM((4, count + 8, size), F32),
            pltpu.VMEM((2, mine, rows), F32), pltpu.VMEM((2, mine, rows), F32),
            pltpu.VMEM((group, 4, mine, size), F32),
            pltpu.VMEM((group, 4, mine, size), BF16), pltpu.VMEM((group, 4, mine, size), BF16),
            sums, pieces, pieces, sums, turns, turns, pieces,
            pltpu.VMEM((count, size), F32), pltpu.VMEM((count, rows), F32),
        ]
        + [dma((group,))] * 2 + [dma((2,))] * 4 + [dma((3,))] * 2
        + [dma((chains, group))] * 2 + [dma((chains, 2))] * 2 + [dma((chains, group))] * 2
        + [dma((2, chains))] * 2,
        compiler_params=pltpu.CompilerParams(
            collective_id=0, has_side_effects=True, vmem_limit_bytes=room
        ),
    )(
        high.reshape(blocks, rows, size), low.reshape(blocks, rows, size),
        primal_start, objective, upper_bound.reshape(1, -1), dual_start, row_bound,
    )


def solution(mesh):
    rows = P(("parts", "row"), None)
    flat = P(("parts", "row"))
    return jax.shard_map(
        body,
        mesh=mesh,
        in_specs=(P(("parts", "row"), None, None), flat, flat, rows, rows, flat, rows, rows),
        out_specs=(rows, rows),
        check_vma=False,
    )
```

```python
import functools

import jax
import jax.numpy as jnp
from jax import lax
from jax.experimental import pallas as pl
from jax.experimental.pallas import tpu as pltpu
from jax.sharding import PartitionSpec as P

ITERS = 3
CHAINS = 2
STEP = 0.4
F32 = jnp.float32
BF16 = jnp.bfloat16


def finish_kernel(primal, dual, primal_out, dual_out):
    primal_out[...] = primal[...].T
    dual_out[...] = dual[...].T


def order_tiles(tile_row, tile_col, table, row_blocks):
    tiles = tile_row.shape[1]
    lanes = table.shape[1]
    across = tile_col[...] * row_blocks + tile_row[...]
    s = lax.broadcasted_iota(jnp.int32, (tiles, tiles), 0)
    t = lax.broadcasted_iota(jnp.int32, (tiles, tiles), 1)
    across = jnp.broadcast_to(across, (tiles, tiles))
    down = jnp.sum(jnp.where(s == t, across, 0), axis=1, keepdims=True)
    before = jnp.logical_or(across < down, jnp.logical_and(across == down, t < s))
    rank = jnp.sum(before.astype(jnp.int32), axis=1, keepdims=True)
    lane = lax.broadcasted_iota(jnp.int32, (tiles, lanes), 1)
    index = lax.broadcasted_iota(jnp.int32, (tiles, lanes), 0)
    here = rank == lane
    table[0:1, :] = jnp.sum(jnp.where(here, index, 0), axis=0, keepdims=True)
    table[1:2, :] = jnp.sum(jnp.where(here, down, 0), axis=0, keepdims=True)
    below = jnp.sum((down <= lane).astype(jnp.int32), axis=0, keepdims=True)
    equal = jnp.sum((down == lane).astype(jnp.int32), axis=0, keepdims=True)
    table[2:3, :] = jnp.where(equal > 0, below - 1, tiles)


def sum_tiles(tiles, order, sums, high, low):
    count, size, _ = tiles.shape
    row_blocks = high.shape[1] // size
    sums[count] = jnp.zeros((size, size), F32)

    def add(r, total):
        again = order[1, r] == order[1, jnp.maximum(r - 1, 0)]
        total = jnp.where(again, total, 0.0) + tiles[order[0, r]].astype(F32)
        sums[r] = total
        return total

    lax.fori_loop(0, count, add, jnp.zeros((size, size), F32), unroll=4)

    @pl.loop(0, high.shape[0], unroll=2)
    def _(c):
        for k in range(row_blocks):
            value = sums[order[2, c * row_blocks + k]]
            rounded = value.astype(BF16)
            high[c, k * size : (k + 1) * size] = rounded
            low[c, k * size : (k + 1) * size] = (value - rounded.astype(F32)).astype(BF16)


def iterate_kernel(
    n, chains, tiles_in, tile_row_in, tile_col_in, primal_in, objective_in, upper_in, dual_in,
    bound_in, primal_end, dual_end,
    tiles, tile_row, tile_col, primal_start, objective, upper, dual_start, row_bound,
    table, order, summed, high, low, far_high, far_low, flipped, bounds, packed, state, dual, bound,
    part_own, part_send, part_recv, own, send1, recv1, half, send2, recv2, spread,
    sl, st, sp, rp, sa, ra, sd, rd, si, ri, s1, r1, s2, r2, sx, rx, se, re,
):
    me = lax.axis_index("row")
    core = lax.rem(me, 2)
    chip = me // 2
    group = n // 4
    side = chip // group
    seat = lax.rem(chip, group)
    partner = me + 1 - 2 * core
    mirror = lax.rem(chip + group, 2 * group) * 2
    size = primal_in.shape[0]
    rows = dual_in.shape[0]
    mine = primal_in.shape[1] // 2
    part = mine // chains
    slot = 2 * side

    def seat_at(d):
        return lax.bitwise_xor(seat, d)

    def peer(d):
        return (side * group + seat_at(d)) * 2 + core

    def send(src, dst, send_sem, recv_sem, device):
        return pltpu.make_async_remote_copy(
            src_ref=src, dst_ref=dst, send_sem=send_sem, recv_sem=recv_sem,
            device_id={"row": device}, device_id_type=pl.DeviceIdType.MESH,
        )

    def whole(h):
        return pl.ds(h * mine, mine)

    def chain(c):
        return pl.ds(c * part, part)

    def place(c):
        return pl.ds(core * mine + c * part, part)

    def load(k):
        src, dst = (
            (tile_col_in, tile_col), (tile_row_in, tile_row), (dual_in, dual_start),
            (tiles_in, tiles), (primal_in, primal_start), (objective_in, objective),
            (upper_in, upper), (bound_in, row_bound),
        )[k]
        return pltpu.make_async_copy(src, dst, sl.at[k])

    def first_partial(c, d):
        return send(
            part_send.at[c, d], part_recv.at[c, d], sp.at[c, d], rp.at[c, d], partner
        )

    def matrix(k):
        src, dst = ((high, far_high), (low, far_low))[k]
        return send(src, dst, sa.at[k], ra.at[k], partner)

    def rows_over(k):
        src, dst = ((flipped, dual), (bounds, bound))[k]
        return send(src.at[whole(1 - core)], dst.at[1], sd.at[k], rd.at[k], partner)

    def start_state(k):
        source = packed.at[core if k == 1 else 1 - core]
        device = (partner, mirror + core, mirror + 1 - core)[k]
        return send(source, state.at[slot + core], si.at[k], ri.at[k], device)

    def reduce(c, d):
        return send(send1.at[c, d], recv1.at[c, d], s1.at[c, d], r1.at[c, d], peer(d))

    def cross(c, step):
        turn = lax.rem(step, 2)
        return send(
            send2.at[c, turn], recv2.at[c, turn], s2.at[c, turn], r2.at[c, turn], mirror + core
        )

    def gather(c, d):
        return send(spread.at[c, 0], spread.at[c, d], sx.at[c, d], rx.at[c, d], peer(d))

    def primal_back(c):
        return send(
            state.at[slot + 1 - core, chain(c)], primal_end.at[place(c)],
            se.at[0, c], re.at[0, c], partner,
        )

    def dual_back(c):
        return send(
            dual.at[1, chain(c)], dual_end.at[place(c)], se.at[1, c], re.at[1, c], partner
        )

    far_first = list(range(group - 1, 0, -1))
    near_first = list(range(1, group))

    def owned(d):
        q = seat_at(d)
        return [2 * q, 2 * q + 1, 2 * (q + group), 2 * (q + group) + 1]

    def dot(left, right, axis):
        return lax.dot_general(
            left, right, (((1,), (axis,)), ((), ())), preferred_element_type=F32
        )

    def side_by_side(ref, blocks):
        return jnp.concatenate([ref[b] for b in blocks], axis=1)

    def columns(left, blocks, pairs):
        total = None
        for refs in pairs:
            right = jnp.concatenate([side_by_side(ref, blocks) for ref in refs], axis=0)
            value = dot(left, right, 0)
            total = value if total is None else total + value
        return total

    near = ((high,), (low,))
    both = ((high, far_high), (low, far_low))

    def start():
        left = jnp.concatenate([flipped[whole(core), :], flipped[whole(1 - core), :]], axis=0)
        left = left.astype(BF16)
        for d in far_first + [0]:
            blocks = owned(d)
            for i in range(0, 4, 2):
                value = columns(left, blocks[i : i + 2], near)
                for k in range(2):
                    piece = value[:, k * size : (k + 1) * size]
                    for c in range(chains):
                        at = c * part
                        part_own[c, d, i + k] = piece[at : at + part]
                        part_send[c, d, i + k] = piece[mine + at : mine + at + part].astype(BF16)

    def finish_start():
        for c in range(chains):
            for d in far_first + [0]:
                first_partial(c, d).wait_recv()
                value = part_own[c, d] + part_recv[c, d].astype(F32)
                if d:
                    send1[c, d] = value.astype(BF16)
                    reduce(c, d).start()
                else:
                    own[c] = value

    def partials(c):
        left = jnp.concatenate([dual[0, chain(c), :], dual[1, chain(c), :]], axis=1)
        left = left.astype(BF16)
        for d in far_first + [0]:
            blocks = owned(d)
            for i in range(0, 4, 2):
                value = columns(left, blocks[i : i + 2], both)
                for k in range(2):
                    piece = value[:, k * size : (k + 1) * size]
                    if d:
                        send1[c, d, i + k] = piece.astype(BF16)
                    else:
                        own[c, i + k] = piece
            if d:
                reduce(c, d).start()

    def merge(c, step):
        total = own[c]
        for d in near_first:
            reduce(c, d).wait_recv()
            total += recv1[c, d].astype(F32)
        half[c] = total
        send2[c, lax.rem(step, 2)] = total.astype(BF16)
        cross(c, step).start()

    def update(c, step):
        cross(c, step).wait_recv()
        total = half[c] + recv2[c, lax.rem(step, 2)].astype(F32)
        before = state[:, chain(c), :]
        cost = state[:, pl.ds(mine + c * part, part), :]
        upper_here = state[:, pl.ds(2 * mine, 1), :]
        updated = jnp.clip(before - STEP * (cost - total), 0.0, upper_here)
        spread[c, 0] = (2.0 * updated - before).astype(BF16)
        for d in far_first:
            gather(c, d).start()
        state[:, chain(c), :] = updated
        for d in near_first:
            reduce(c, d).wait_send()
        cross(c, step).wait_send()

    def image(c):
        total = None
        for d in [0] + near_first:
            if d:
                gather(c, d).wait_recv()
            blocks = owned(d)
            left = jnp.concatenate([spread[c, d, i] for i in range(4)], axis=1)
            for refs in both:
                right = jnp.concatenate([side_by_side(ref, blocks) for ref in refs], axis=0)
                value = dot(left, right, 1)
                total = value if total is None else total + value
        for k in range(2):
            dual[k, chain(c), :] = jnp.maximum(
                dual[k, chain(c), :]
                + STEP * (bound[k, chain(c), :] - total[:, k * rows : (k + 1) * rows]),
                0.0,
            )
        for d in near_first:
            gather(c, d).wait_send()

    barrier = pltpu.get_barrier_semaphore()
    others = [partner, mirror + core, mirror + 1 - core] + [peer(d) for d in near_first]
    for other in others:
        pl.semaphore_signal(
            barrier, inc=1, device_id={"row": other}, device_id_type=pl.DeviceIdType.MESH
        )
    for k in range(8):
        load(k).start()
    load(0).wait()
    load(1).wait()
    order_tiles(tile_row, tile_col, table, rows // size)
    to_scalars = pltpu.make_async_copy(table, order, st)
    to_scalars.start()
    load(2).wait()
    flipped[...] = dual_start[...].T
    to_scalars.wait()
    load(3).wait()
    sum_tiles(tiles, order, summed, high, low)
    start()
    for k in range(4, 8):
        load(k).wait()
    for source, offset in ((primal_start, 0), (objective, mine)):
        value = source[...].T
        for h in range(2):
            packed[h, pl.ds(offset, mine), :] = value[h * mine : (h + 1) * mine]
    for h in range(2):
        packed[h, pl.ds(2 * mine, 8), :] = jnp.broadcast_to(upper[...], (8, size))
    bounds[...] = row_bound[...].T
    pl.semaphore_wait(barrier, len(others))
    for c in range(chains):
        for d in far_first + [0]:
            first_partial(c, d).start()
    for k in (1, 2, 0):
        start_state(k).start()
    for k in range(2):
        rows_over(k).start()
    for k in range(2):
        matrix(k).start()
    state[slot + core] = packed[core]
    dual[0] = flipped[whole(core), :]
    bound[0] = bounds[whole(core), :]
    finish_start()
    for c in range(chains):
        merge(c, 0)
    for k in range(3):
        start_state(k).wait()
    for k in range(2):
        rows_over(k).wait()
        matrix(k).wait()
    for c in range(chains):
        for d in range(group):
            first_partial(c, d).wait_send()

    def iteration(step, carry):
        more = step < ITERS - 1
        for c in range(chains):
            update(c, step)

            @pl.when(jnp.logical_not(more))
            def _():
                primal_back(c).start()

        for c in range(chains):
            image(c)
            pl.when(more)(functools.partial(partials, c))

            @pl.when(jnp.logical_not(more))
            def _():
                dual_back(c).start()

        @pl.when(more)
        def _():
            for c in range(chains):
                merge(c, step + 1)

        return carry

    lax.fori_loop(0, ITERS, iteration, 0)
    for c in range(chains):
        primal_end[place(c), :] = state[slot + core, chain(c), :]
        dual_end[place(c), :] = dual[0, chain(c), :]
    for c in range(chains):
        primal_back(c).wait()
        dual_back(c).wait()


def body(
    tile_values, tile_row, tile_col, primal_start, objective, upper_bound, dual_start, row_bound
):
    n = lax.axis_size("row")
    size = tile_values.shape[1]
    count = primal_start.shape[1]
    blocks = n * primal_start.shape[0] // size
    group = n // 4
    assert blocks == n and n % 4 == 0 and group & (group - 1) == 0
    rows = dual_start.shape[0]
    row_blocks = rows // size
    tiles = tile_values.shape[0]
    chains = CHAINS
    mine = count // 2
    part = mine // chains
    lanes = -(-max(tiles, blocks * row_blocks) // 128) * 128
    vmem = pl.BlockSpec(memory_space=pltpu.VMEM)
    dma = pltpu.SemaphoreType.DMA
    matrix = pltpu.VMEM((blocks, rows, size), BF16)
    column = pltpu.VMEM(primal_start.shape, F32)
    row = pltpu.VMEM(dual_start.shape, F32)
    pieces = pltpu.VMEM((chains, group, 4, part, size), BF16)
    sums = pltpu.VMEM((chains, 4, part, size), F32)
    turns = pltpu.VMEM((chains, 2, 4, part, size), BF16)
    room = (
        8 * blocks * rows * size + 6 * (tiles + 1) * size * size
        + 32 * blocks * mine * size + (8 << 20)
    )
    primal_end, dual_end = pl.pallas_call(
        functools.partial(iterate_kernel, n, chains),
        out_shape=(
            jax.ShapeDtypeStruct((count, size), F32), jax.ShapeDtypeStruct((count, rows), F32)
        ),
        in_specs=[pl.BlockSpec(memory_space=pltpu.HBM)] * 8,
        out_specs=(vmem, vmem),
        scratch_shapes=[
            pltpu.VMEM(tile_values.shape, BF16),
            pltpu.VMEM((1, tiles), jnp.int32), pltpu.VMEM((1, tiles), jnp.int32),
            column, column, pltpu.VMEM((1, size), F32), row, row,
            pltpu.VMEM((8, lanes), jnp.int32), pltpu.SMEM((8, lanes), jnp.int32),
            pltpu.VMEM((tiles + 1, size, size), F32),
            matrix, matrix, matrix, matrix,
            pltpu.VMEM((count, rows), F32), pltpu.VMEM((count, rows), F32),
            pltpu.VMEM((2, count + 8, size), F32), pltpu.VMEM((4, count + 8, size), F32),
            pltpu.VMEM((2, mine, rows), F32), pltpu.VMEM((2, mine, rows), F32),
            pltpu.VMEM((chains, group, 4, part, size), F32), pieces, pieces,
            sums, pieces, pieces, sums, turns, turns, pieces,
            dma((8,)), dma(()),
        ]
        + [dma((chains, group))] * 2 + [dma((2,))] * 4 + [dma((3,))] * 2
        + [dma((chains, group))] * 2 + [dma((chains, 2))] * 2 + [dma((chains, group))] * 2
        + [dma((2, chains))] * 2,
        compiler_params=pltpu.CompilerParams(
            collective_id=0, has_side_effects=True, vmem_limit_bytes=room
        ),
    )(
        tile_values, tile_row.reshape(1, -1), tile_col.reshape(1, -1), primal_start, objective,
        upper_bound.reshape(1, -1), dual_start, row_bound,
    )
    return pl.pallas_call(
        finish_kernel,
        out_shape=(
            jax.ShapeDtypeStruct(primal_start.shape, F32),
            jax.ShapeDtypeStruct(dual_start.shape, F32),
        ),
        in_specs=[vmem] * 2,
        out_specs=(vmem, vmem),
    )(primal_end, dual_end)


def solution(mesh):
    rows = P(("parts", "row"), None)
    flat = P(("parts", "row"))
    return jax.shard_map(
        body,
        mesh=mesh,
        in_specs=(P(("parts", "row"), None, None), flat, flat, rows, rows, flat, rows, rows),
        out_specs=(rows, rows),
        check_vma=False,
    )
```

```python
import functools

import jax
import jax.numpy as jnp
from jax import lax
from jax.experimental import pallas as pl
from jax.experimental.pallas import tpu as pltpu
from jax.sharding import PartitionSpec as P

ITERS = 3
CHAINS = 2
STEP = 0.4
F32 = jnp.float32
BF16 = jnp.bfloat16


def finish_kernel(primal, dual, primal_out, dual_out):
    primal_out[...] = primal[...].T
    dual_out[...] = dual[...].T


def order_tiles(tile_row, tile_col, table, row_blocks):
    tiles = tile_row.shape[1]
    lanes = table.shape[1]
    across = tile_col[...] * row_blocks + tile_row[...]
    s = lax.broadcasted_iota(jnp.int32, (tiles, tiles), 0)
    t = lax.broadcasted_iota(jnp.int32, (tiles, tiles), 1)
    across = jnp.broadcast_to(across, (tiles, tiles))
    down = jnp.sum(jnp.where(s == t, across, 0), axis=1, keepdims=True)
    before = jnp.logical_or(across < down, jnp.logical_and(across == down, t < s))
    rank = jnp.sum(before.astype(jnp.int32), axis=1, keepdims=True)
    lane = lax.broadcasted_iota(jnp.int32, (tiles, lanes), 1)
    index = lax.broadcasted_iota(jnp.int32, (tiles, lanes), 0)
    here = rank == lane
    table[0:1, :] = jnp.sum(jnp.where(here, index, 0), axis=0, keepdims=True)
    table[1:2, :] = jnp.sum(jnp.where(here, down, 0), axis=0, keepdims=True)
    below = jnp.sum((down <= lane).astype(jnp.int32), axis=0, keepdims=True)
    equal = jnp.sum((down == lane).astype(jnp.int32), axis=0, keepdims=True)
    table[2:3, :] = jnp.where(equal > 0, below - 1, tiles)


def sum_tiles(tiles, order, sums, high, low):
    count, size, _ = tiles.shape
    row_blocks = high.shape[1] // size
    sums[count] = jnp.zeros((size, size), F32)

    def add(r, total):
        again = order[1, r] == order[1, jnp.maximum(r - 1, 0)]
        total = jnp.where(again, total, 0.0) + tiles[order[0, r]].astype(F32)
        sums[r] = total
        return total

    lax.fori_loop(0, count, add, jnp.zeros((size, size), F32), unroll=4)

    @pl.loop(0, high.shape[0], unroll=2)
    def _(c):
        for k in range(row_blocks):
            value = sums[order[2, c * row_blocks + k]]
            rounded = value.astype(BF16)
            high[c, k * size : (k + 1) * size] = rounded
            low[c, k * size : (k + 1) * size] = (value - rounded.astype(F32)).astype(BF16)


def iterate_kernel(
    n, chains, tiles_in, tile_row_in, tile_col_in, primal_in, objective_in, upper_in, dual_in,
    bound_in, primal_end, dual_end,
    tiles, tile_row, tile_col, primal_start, objective, upper, dual_start, row_bound,
    table, order, summed, high, low, far_high, far_low, high_turned, low_turned,
    flipped, bounds, packed, state, dual, bound,
    part_own, part_send, part_recv, own, send1, recv1, spread,
    sl, st, sp, rp, sa, ra, sd, rd, si, ri, s1, r1, sx, rx, se, re,
):
    me = lax.axis_index("row")
    core = lax.rem(me, 2)
    chip = me // 2
    chips = n // 2
    partner = me + 1 - 2 * core
    size = primal_in.shape[0]
    rows = dual_in.shape[0]
    mine = primal_in.shape[1] // 2
    part = mine // chains

    def chip_at(d):
        return lax.bitwise_xor(chip, d)

    def peer(d):
        return chip_at(d) * 2 + core

    def send(src, dst, send_sem, recv_sem, device):
        return pltpu.make_async_remote_copy(
            src_ref=src, dst_ref=dst, send_sem=send_sem, recv_sem=recv_sem,
            device_id={"row": device}, device_id_type=pl.DeviceIdType.MESH,
        )

    def whole(h):
        return pl.ds(h * mine, mine)

    def chain(c):
        return pl.ds(c * part, part)

    def place(c):
        return pl.ds(core * mine + c * part, part)

    def load(k):
        src, dst = (
            (tile_col_in, tile_col), (tile_row_in, tile_row), (dual_in, dual_start),
            (tiles_in, tiles), (primal_in, primal_start), (objective_in, objective),
            (upper_in, upper), (bound_in, row_bound),
        )[k]
        return pltpu.make_async_copy(src, dst, sl.at[k])

    def first_partial(c, d):
        return send(
            part_send.at[c, d], part_recv.at[c, d], sp.at[c, d], rp.at[c, d], partner
        )

    def matrix(k):
        src, dst = ((high, far_high), (low, far_low))[k]
        return send(src, dst, sa.at[k], ra.at[k], partner)

    def rows_over(k):
        src, dst = ((flipped, dual), (bounds, bound))[k]
        return send(src.at[whole(1 - core)], dst.at[1], sd.at[k], rd.at[k], partner)

    def start_state():
        return send(packed.at[1 - core], state.at[core], si, ri, partner)

    def reduce(c, d):
        return send(send1.at[c, d], recv1.at[c, d], s1.at[c, d], r1.at[c, d], peer(d))

    def gather(c, d):
        return send(spread.at[c, 0], spread.at[c, d], sx.at[c, d], rx.at[c, d], peer(d))

    def primal_back(c):
        return send(
            state.at[1 - core, chain(c)], primal_end.at[place(c)], se.at[0, c], re.at[0, c], partner
        )

    def dual_back(c):
        return send(
            dual.at[1, chain(c)], dual_end.at[place(c)], se.at[1, c], re.at[1, c], partner
        )

    far_first = list(range(chips - 1, 0, -1))
    near_first = list(range(1, chips))

    def dot(left, right):
        return lax.dot_general(
            left, right, (((1,), (0,)), ((), ())), preferred_element_type=F32
        )

    def columns(left, d, pairs):
        q = 2 * chip_at(d)
        total = None
        for refs in pairs:
            right = jnp.concatenate(
                [jnp.concatenate([ref[q], ref[q + 1]], axis=1) for ref in refs], axis=0
            )
            value = dot(left, right)
            total = value if total is None else total + value
        return [total[:, k * size : (k + 1) * size] for k in range(2)]

    def start():
        left = jnp.concatenate([flipped[whole(core), :], flipped[whole(1 - core), :]], axis=0)
        left = left.astype(BF16)
        for d in far_first + [0]:
            for k, piece in enumerate(columns(left, d, ((high,), (low,)))):
                for c in range(chains):
                    at = c * part
                    part_own[c, d, k] = piece[at : at + part]
                    part_send[c, d, k] = piece[mine + at : mine + at + part].astype(BF16)

    def finish_start():
        for c in range(chains):
            for d in far_first + [0]:
                first_partial(c, d).wait_recv()
                value = part_own[c, d] + part_recv[c, d].astype(F32)
                if d:
                    send1[c, d] = value.astype(BF16)
                    reduce(c, d).start()
                else:
                    own[c] = value

    def turn(pairs, at):
        @pl.loop(0, high.shape[0], unroll=4)
        def _(b):
            for source, target in pairs:
                target[b, :, at : at + rows] = source[b].T

    def partials(c):
        left = jnp.concatenate([dual[0, chain(c), :], dual[1, chain(c), :]], axis=1)
        left = left.astype(BF16)
        for d in far_first + [0]:
            for k, piece in enumerate(columns(left, d, ((high, far_high), (low, far_low)))):
                if d:
                    send1[c, d, k] = piece.astype(BF16)
                else:
                    own[c, k] = piece
            if d:
                reduce(c, d).start()

    def update(c):
        total = own[c]
        for d in near_first:
            reduce(c, d).wait_recv()
            total += recv1[c, d].astype(F32)
        before = state[:, chain(c), :]
        cost = state[:, pl.ds(mine + c * part, part), :]
        upper_here = state[:, pl.ds(2 * mine, 1), :]
        updated = jnp.clip(before - STEP * (cost - total), 0.0, upper_here)
        spread[c, 0] = (2.0 * updated - before).astype(BF16)
        for d in far_first:
            gather(c, d).start()
        state[:, chain(c), :] = updated
        for d in near_first:
            reduce(c, d).wait_send()

    def image(c):
        total = None
        for d in [0] + near_first:
            if d:
                gather(c, d).wait_recv()
            q = 2 * chip_at(d)
            left = jnp.concatenate([spread[c, d, k] for k in range(2)], axis=1)
            for ref in (high_turned, low_turned):
                right = jnp.concatenate([ref[q], ref[q + 1]], axis=0)
                value = dot(left, right)
                total = value if total is None else total + value
        for k in range(2):
            dual[k, chain(c), :] = jnp.maximum(
                dual[k, chain(c), :]
                + STEP * (bound[k, chain(c), :] - total[:, k * rows : (k + 1) * rows]),
                0.0,
            )
        for d in near_first:
            gather(c, d).wait_send()

    barrier = pltpu.get_barrier_semaphore()
    others = [partner] + [peer(d) for d in near_first]
    for other in others:
        pl.semaphore_signal(
            barrier, inc=1, device_id={"row": other}, device_id_type=pl.DeviceIdType.MESH
        )
    for k in range(8):
        load(k).start()
    load(0).wait()
    load(1).wait()
    order_tiles(tile_row, tile_col, table, rows // size)
    to_scalars = pltpu.make_async_copy(table, order, st)
    to_scalars.start()
    load(2).wait()
    flipped[...] = dual_start[...].T
    to_scalars.wait()
    load(3).wait()
    sum_tiles(tiles, order, summed, high, low)
    start()
    pl.semaphore_wait(barrier, len(others))
    for c in range(chains):
        for d in far_first + [0]:
            first_partial(c, d).start()
    for k in range(4, 8):
        load(k).wait()
    for source, offset in ((primal_start, 0), (objective, mine)):
        value = source[...].T
        for h in range(2):
            packed[h, pl.ds(offset, mine), :] = value[h * mine : (h + 1) * mine]
    for h in range(2):
        packed[h, pl.ds(2 * mine, 8), :] = jnp.broadcast_to(upper[...], (8, size))
    bounds[...] = row_bound[...].T
    finish_start()
    start_state().start()
    for k in range(2):
        rows_over(k).start()
    for k in range(2):
        matrix(k).start()
    state[core] = packed[core]
    dual[0] = flipped[whole(core), :]
    bound[0] = bounds[whole(core), :]
    turn(((high, high_turned), (low, low_turned)), 0)
    start_state().wait()
    for k in range(2):
        rows_over(k).wait()
        matrix(k).wait()
    turn(((far_high, high_turned), (far_low, low_turned)), rows)
    for c in range(chains):
        for d in range(chips):
            first_partial(c, d).wait_send()

    def iteration(step, carry):
        more = step < ITERS - 1
        for c in range(chains):
            update(c)

            @pl.when(jnp.logical_not(more))
            def _():
                primal_back(c).start()

        for c in range(chains):
            image(c)
            pl.when(more)(functools.partial(partials, c))

            @pl.when(jnp.logical_not(more))
            def _():
                dual_back(c).start()

        return carry

    lax.fori_loop(0, ITERS, iteration, 0)
    for c in range(chains):
        primal_end[place(c), :] = state[core, chain(c), :]
        dual_end[place(c), :] = dual[0, chain(c), :]
    for c in range(chains):
        primal_back(c).wait()
        dual_back(c).wait()


def body(
    tile_values, tile_row, tile_col, primal_start, objective, upper_bound, dual_start, row_bound
):
    n = lax.axis_size("row")
    size = tile_values.shape[1]
    count = primal_start.shape[1]
    blocks = n * primal_start.shape[0] // size
    chips = n // 2
    assert blocks == n and n % 2 == 0 and chips & (chips - 1) == 0
    rows = dual_start.shape[0]
    row_blocks = rows // size
    tiles = tile_values.shape[0]
    chains = CHAINS
    mine = count // 2
    part = mine // chains
    lanes = -(-max(tiles, blocks * row_blocks) // 128) * 128
    vmem = pl.BlockSpec(memory_space=pltpu.VMEM)
    dma = pltpu.SemaphoreType.DMA
    matrix = pltpu.VMEM((blocks, rows, size), BF16)
    column = pltpu.VMEM(primal_start.shape, F32)
    row = pltpu.VMEM(dual_start.shape, F32)
    row_flipped = pltpu.VMEM((count, rows), F32)
    turned = pltpu.VMEM((blocks, size, 2 * rows), BF16)
    pieces = pltpu.VMEM((chains, chips, 2, part, size), BF16)
    primal_end, dual_end = pl.pallas_call(
        functools.partial(iterate_kernel, n, chains),
        out_shape=(
            pltpu.VMEM((count, size), F32), pltpu.VMEM((count, rows), F32)
        ),
        in_specs=[pl.BlockSpec(memory_space=pltpu.HBM)] * 8,
        out_specs=(vmem, vmem),
        scratch_shapes=[
            pltpu.VMEM(tile_values.shape, BF16),
            pltpu.VMEM((1, tiles), jnp.int32), pltpu.VMEM((1, tiles), jnp.int32),
            column, column, pltpu.VMEM((1, size), F32), row, row,
            pltpu.VMEM((8, lanes), jnp.int32), pltpu.SMEM((8, lanes), jnp.int32),
            pltpu.VMEM((tiles + 1, size, size), F32),
            matrix, matrix, matrix, matrix, turned, turned,
            row_flipped, row_flipped,
            pltpu.VMEM((2, count + 8, size), F32), pltpu.VMEM((2, count + 8, size), F32),
            pltpu.VMEM((2, mine, rows), F32), pltpu.VMEM((2, mine, rows), F32),
            pltpu.VMEM((chains, chips, 2, part, size), F32), pieces, pieces,
            pltpu.VMEM((chains, 2, part, size), F32), pieces, pieces, pieces,
            dma((8,)), dma(()),
        ]
        + [dma((chains, chips))] * 2 + [dma((2,))] * 4 + [dma(())] * 2
        + [dma((chains, chips))] * 4 + [dma((2, chains))] * 2,
        compiler_params=pltpu.CompilerParams(
            collective_id=0, has_side_effects=True, vmem_limit_bytes=66000000
        ),
    )(
        tile_values, tile_row.reshape(1, -1), tile_col.reshape(1, -1), primal_start, objective,
        upper_bound.reshape(1, -1), dual_start, row_bound,
    )
    return pl.pallas_call(
        finish_kernel,
        out_shape=(
            jax.ShapeDtypeStruct(primal_start.shape, F32),
            jax.ShapeDtypeStruct(dual_start.shape, F32),
        ),
        in_specs=[vmem] * 2,
        out_specs=(vmem, vmem),
        compiler_params=pltpu.CompilerParams(vmem_limit_bytes=1 << 20),
    )(primal_end, dual_end)


def solution(mesh):
    rows = P(("parts", "row"), None)
    flat = P(("parts", "row"))
    return jax.shard_map(
        body,
        mesh=mesh,
        in_specs=(P(("parts", "row"), None, None), flat, flat, rows, rows, flat, rows, rows),
        out_specs=(rows, rows),
        check_vma=False,
    )
```

```python
import functools

import jax
import jax.numpy as jnp
from jax import lax
from jax.experimental import pallas as pl
from jax.experimental.pallas import tpu as pltpu
from jax.sharding import PartitionSpec as P

ITERS = 3
CHAINS = 2
STEP = 0.4
F32 = jnp.float32
BF16 = jnp.bfloat16


def finish_kernel(primal, dual, primal_out, dual_out):
    primal_out[...] = primal[...].T
    dual_out[...] = dual[...].T


def order_tiles(tile_row, tile_col, table, row_blocks):
    tiles = tile_row.shape[1]
    lanes = table.shape[1]
    across = tile_col[...] * row_blocks + tile_row[...]
    s = lax.broadcasted_iota(jnp.int32, (tiles, tiles), 0)
    t = lax.broadcasted_iota(jnp.int32, (tiles, tiles), 1)
    across = jnp.broadcast_to(across, (tiles, tiles))
    down = jnp.sum(jnp.where(s == t, across, 0), axis=1, keepdims=True)
    before = jnp.logical_or(across < down, jnp.logical_and(across == down, t < s))
    rank = jnp.sum(before.astype(jnp.int32), axis=1, keepdims=True)
    lane = lax.broadcasted_iota(jnp.int32, (tiles, lanes), 1)
    index = lax.broadcasted_iota(jnp.int32, (tiles, lanes), 0)
    here = rank == lane
    table[0:1, :] = jnp.sum(jnp.where(here, index, 0), axis=0, keepdims=True)
    table[1:2, :] = jnp.sum(jnp.where(here, down, 0), axis=0, keepdims=True)
    below = jnp.sum((down <= lane).astype(jnp.int32), axis=0, keepdims=True)
    equal = jnp.sum((down == lane).astype(jnp.int32), axis=0, keepdims=True)
    table[2:3, :] = jnp.where(equal > 0, below - 1, tiles)


def sum_tiles(tiles, order, sums, high, low):
    count, size, _ = tiles.shape
    row_blocks = high.shape[1] // size
    sums[count] = jnp.zeros((size, size), F32)

    def add(r, total):
        again = order[1, r] == order[1, jnp.maximum(r - 1, 0)]
        total = jnp.where(again, total, 0.0) + tiles[order[0, r]].astype(F32)
        sums[r] = total
        return total

    lax.fori_loop(0, count, add, jnp.zeros((size, size), F32), unroll=4)

    @pl.loop(0, high.shape[0], unroll=2)
    def _(c):
        for k in range(row_blocks):
            value = sums[order[2, c * row_blocks + k]]
            rounded = value.astype(BF16)
            high[c, k * size : (k + 1) * size] = rounded
            low[c, k * size : (k + 1) * size] = (value - rounded.astype(F32)).astype(BF16)


def iterate_kernel(
    n, chains, tiles_in, tile_row_in, tile_col_in, primal_in, objective_in, upper_in, dual_in,
    bound_in, primal_end, dual_end,
    tiles, tile_row, tile_col, primal_start, objective, upper, dual_start, row_bound,
    table, order, summed, high, low, far_high, far_low, high_turned, low_turned,
    flipped, bounds, packed, state, dual, bound,
    part_own, part_send, part_recv, own, send1, recv1, spread,
    sl, st, sp, rp, sa, ra, sd, rd, si, ri, s1, r1, sx, rx, se, re,
):
    me = lax.axis_index("row")
    core = lax.rem(me, 2)
    chip = me // 2
    chips = n // 2
    partner = me + 1 - 2 * core
    size = primal_in.shape[0]
    rows = dual_in.shape[0]
    mine = primal_in.shape[1] // 2
    part = mine // chains

    def chip_at(d):
        return lax.bitwise_xor(chip, d)

    def peer(d):
        return chip_at(d) * 2 + core

    def send(src, dst, send_sem, recv_sem, device):
        return pltpu.make_async_remote_copy(
            src_ref=src, dst_ref=dst, send_sem=send_sem, recv_sem=recv_sem,
            device_id={"row": device}, device_id_type=pl.DeviceIdType.MESH,
        )

    def whole(h):
        return pl.ds(h * mine, mine)

    def chain(c):
        return pl.ds(c * part, part)

    def place(c):
        return pl.ds(core * mine + c * part, part)

    def load(k):
        src, dst = (
            (tile_col_in, tile_col), (tile_row_in, tile_row), (dual_in, dual_start),
            (tiles_in, tiles), (primal_in, primal_start), (objective_in, objective),
            (upper_in, upper), (bound_in, row_bound),
        )[k]
        return pltpu.make_async_copy(src, dst, sl.at[k])

    def first_partial(c, d):
        return send(
            part_send.at[c, d], part_recv.at[c, d], sp.at[c, d], rp.at[c, d], partner
        )

    def matrix(k):
        src, dst = ((high, far_high), (low, far_low))[k]
        return send(src, dst, sa.at[k], ra.at[k], partner)

    def rows_over(k):
        src, dst = ((flipped, dual), (bounds, bound))[k]
        return send(src.at[whole(1 - core)], dst.at[1], sd.at[k], rd.at[k], partner)

    def start_state():
        return send(packed.at[1 - core], state.at[core], si, ri, partner)

    def reduce(c, d):
        return send(send1.at[c, d], recv1.at[c, d], s1.at[c, d], r1.at[c, d], peer(d))

    def gather(c, d):
        return send(spread.at[c, 0], spread.at[c, d], sx.at[c, d], rx.at[c, d], peer(d))

    def primal_back(c):
        return send(
            state.at[1 - core, chain(c)], primal_end.at[place(c)], se.at[0, c], re.at[0, c], partner
        )

    def dual_back(c):
        return send(
            dual.at[1, chain(c)], dual_end.at[place(c)], se.at[1, c], re.at[1, c], partner
        )

    far_first = [*range(chips - 1, 1, -2), *range(chips - 2, 0, -2), 1]
    near_first = list(range(1, chips))

    def dot(left, right):
        return lax.dot_general(
            left, right, (((1,), (0,)), ((), ())), preferred_element_type=F32
        )

    def columns(left, d, pairs):
        q = 2 * chip_at(d)
        total = None
        for refs in pairs:
            right = jnp.concatenate(
                [jnp.concatenate([ref[q], ref[q + 1]], axis=1) for ref in refs], axis=0
            )
            value = dot(left, right)
            total = value if total is None else total + value
        return [total[:, k * size : (k + 1) * size] for k in range(2)]

    def start():
        left = jnp.concatenate([flipped[whole(core), :], flipped[whole(1 - core), :]], axis=0)
        left = left.astype(BF16)
        for d in far_first + [0]:
            for k, piece in enumerate(columns(left, d, ((high,), (low,)))):
                for c in range(chains):
                    at = c * part
                    part_own[c, d, k] = piece[at : at + part]
                    part_send[c, d, k] = piece[mine + at : mine + at + part].astype(BF16)
            for c in range(chains):
                first_partial(c, d).start()

    def finish_start():
        for c in range(chains):
            for d in far_first + [0]:
                first_partial(c, d).wait_recv()
                value = part_own[c, d] + part_recv[c, d].astype(F32)
                if d:
                    send1[c, d] = value.astype(BF16)
                    reduce(c, d).start()
                else:
                    own[c] = value

    def turn(pairs, at):
        @pl.loop(0, high.shape[0], unroll=4)
        def _(b):
            for source, target in pairs:
                target[b, :, at : at + rows] = source[b].T

    def partials(c):
        left = jnp.concatenate([dual[0, chain(c), :], dual[1, chain(c), :]], axis=1)
        left = left.astype(BF16)
        for d in far_first + [0]:
            for k, piece in enumerate(columns(left, d, ((high, far_high), (low, far_low)))):
                if d:
                    send1[c, d, k] = piece.astype(BF16)
                else:
                    own[c, k] = piece
            if d:
                reduce(c, d).start()

    def update(c):
        total = own[c]
        for d in near_first:
            reduce(c, d).wait_recv()
            total += recv1[c, d].astype(F32)
        before = state[:, chain(c), :]
        cost = state[:, pl.ds(mine + c * part, part), :]
        upper_here = state[:, pl.ds(2 * mine, 1), :]
        updated = jnp.clip(before - STEP * (cost - total), 0.0, upper_here)
        spread[c, 0] = (2.0 * updated - before).astype(BF16)
        for d in far_first:
            gather(c, d).start()
        state[:, chain(c), :] = updated
        for d in near_first:
            reduce(c, d).wait_send()

    def image(c):
        total = None
        for d in [0] + near_first:
            if d:
                gather(c, d).wait_recv()
            q = 2 * chip_at(d)
            left = jnp.concatenate([spread[c, d, k] for k in range(2)], axis=1)
            for ref in (high_turned, low_turned):
                right = jnp.concatenate([ref[q], ref[q + 1]], axis=0)
                value = dot(left, right)
                total = value if total is None else total + value
        for k in range(2):
            dual[k, chain(c), :] = jnp.maximum(
                dual[k, chain(c), :]
                + STEP * (bound[k, chain(c), :] - total[:, k * rows : (k + 1) * rows]),
                0.0,
            )
        for d in near_first:
            gather(c, d).wait_send()

    barrier = pltpu.get_barrier_semaphore()
    others = [partner] + [peer(d) for d in near_first]
    for other in others:
        pl.semaphore_signal(
            barrier, inc=1, device_id={"row": other}, device_id_type=pl.DeviceIdType.MESH
        )
    for k in range(8):
        load(k).start()
    load(0).wait()
    load(1).wait()
    order_tiles(tile_row, tile_col, table, rows // size)
    to_scalars = pltpu.make_async_copy(table, order, st)
    to_scalars.start()
    load(2).wait()
    flipped[...] = dual_start[...].T
    to_scalars.wait()
    load(3).wait()
    sum_tiles(tiles, order, summed, high, low)
    pl.semaphore_wait(barrier, len(others))
    start()
    for k in range(4, 8):
        load(k).wait()
    for source, offset in ((primal_start, 0), (objective, mine)):
        value = source[...].T
        for h in range(2):
            packed[h, pl.ds(offset, mine), :] = value[h * mine : (h + 1) * mine]
    for h in range(2):
        packed[h, pl.ds(2 * mine, 8), :] = jnp.broadcast_to(upper[...], (8, size))
    bounds[...] = row_bound[...].T
    finish_start()
    start_state().start()
    for k in range(2):
        rows_over(k).start()
    for k in range(2):
        matrix(k).start()
    state[core] = packed[core]
    dual[0] = flipped[whole(core), :]
    bound[0] = bounds[whole(core), :]
    turn(((high, high_turned), (low, low_turned)), 0)
    start_state().wait()
    for k in range(2):
        rows_over(k).wait()
        matrix(k).wait()
    turn(((far_high, high_turned), (far_low, low_turned)), rows)
    for c in range(chains):
        for d in range(chips):
            first_partial(c, d).wait_send()

    def iteration(step, carry):
        more = step < ITERS - 1
        for c in range(chains):
            update(c)

            @pl.when(jnp.logical_not(more))
            def _():
                primal_back(c).start()

        for c in range(chains):
            image(c)
            pl.when(more)(functools.partial(partials, c))

            @pl.when(jnp.logical_not(more))
            def _():
                dual_back(c).start()

        return carry

    lax.fori_loop(0, ITERS, iteration, 0)
    for c in range(chains):
        primal_end[place(c), :] = state[core, chain(c), :]
        dual_end[place(c), :] = dual[0, chain(c), :]
    for c in range(chains):
        primal_back(c).wait()
        dual_back(c).wait()


def body(
    tile_values, tile_row, tile_col, primal_start, objective, upper_bound, dual_start, row_bound
):
    n = lax.axis_size("row")
    size = tile_values.shape[1]
    count = primal_start.shape[1]
    blocks = n * primal_start.shape[0] // size
    chips = n // 2
    assert blocks == n and n % 2 == 0 and chips & (chips - 1) == 0
    rows = dual_start.shape[0]
    row_blocks = rows // size
    tiles = tile_values.shape[0]
    chains = CHAINS
    mine = count // 2
    part = mine // chains
    lanes = -(-max(tiles, blocks * row_blocks) // 128) * 128
    vmem = pl.BlockSpec(memory_space=pltpu.VMEM)
    dma = pltpu.SemaphoreType.DMA
    matrix = pltpu.VMEM((blocks, rows, size), BF16)
    column = pltpu.VMEM(primal_start.shape, F32)
    row = pltpu.VMEM(dual_start.shape, F32)
    row_flipped = pltpu.VMEM((count, rows), F32)
    turned = pltpu.VMEM((blocks, size, 2 * rows), BF16)
    pieces = pltpu.VMEM((chains, chips, 2, part, size), BF16)
    primal_end, dual_end = pl.pallas_call(
        functools.partial(iterate_kernel, n, chains),
        out_shape=(
            pltpu.VMEM((count, size), F32), pltpu.VMEM((count, rows), F32)
        ),
        in_specs=[pl.BlockSpec(memory_space=pltpu.HBM)] * 8,
        out_specs=(vmem, vmem),
        scratch_shapes=[
            pltpu.VMEM(tile_values.shape, BF16),
            pltpu.VMEM((1, tiles), jnp.int32), pltpu.VMEM((1, tiles), jnp.int32),
            column, column, pltpu.VMEM((1, size), F32), row, row,
            pltpu.VMEM((8, lanes), jnp.int32), pltpu.SMEM((8, lanes), jnp.int32),
            pltpu.VMEM((tiles + 1, size, size), F32),
            matrix, matrix, matrix, matrix, turned, turned,
            row_flipped, row_flipped,
            pltpu.VMEM((2, count + 8, size), F32), pltpu.VMEM((2, count + 8, size), F32),
            pltpu.VMEM((2, mine, rows), F32), pltpu.VMEM((2, mine, rows), F32),
            pltpu.VMEM((chains, chips, 2, part, size), F32), pieces, pieces,
            pltpu.VMEM((chains, 2, part, size), F32), pieces, pieces, pieces,
            dma((8,)), dma(()),
        ]
        + [dma((chains, chips))] * 2 + [dma((2,))] * 4 + [dma(())] * 2
        + [dma((chains, chips))] * 4 + [dma((2, chains))] * 2,
        compiler_params=pltpu.CompilerParams(
            collective_id=0, has_side_effects=True, vmem_limit_bytes=66000000
        ),
    )(
        tile_values, tile_row.reshape(1, -1), tile_col.reshape(1, -1), primal_start, objective,
        upper_bound.reshape(1, -1), dual_start, row_bound,
    )
    return pl.pallas_call(
        finish_kernel,
        out_shape=(
            jax.ShapeDtypeStruct(primal_start.shape, F32),
            jax.ShapeDtypeStruct(dual_start.shape, F32),
        ),
        in_specs=[vmem] * 2,
        out_specs=(vmem, vmem),
        compiler_params=pltpu.CompilerParams(vmem_limit_bytes=1 << 20),
    )(primal_end, dual_end)


def solution(mesh):
    rows = P(("parts", "row"), None)
    flat = P(("parts", "row"))
    return jax.shard_map(
        body,
        mesh=mesh,
        in_specs=(P(("parts", "row"), None, None), flat, flat, rows, rows, flat, rows, rows),
        out_specs=(rows, rows),
        check_vma=False,
    )
```

```python
import functools

import jax
import jax.numpy as jnp
from jax import lax
from jax.experimental import pallas as pl
from jax.experimental.pallas import tpu as pltpu
from jax.sharding import PartitionSpec as P

ITERS = 3
CHAINS = 2
PIECES = 1
STEP = 0.4
F32 = jnp.float32
BF16 = jnp.bfloat16


def finish_kernel(primal, dual, primal_out, dual_out):
    primal_out[...] = primal[...].T
    dual_out[...] = dual[...].T


def order_tiles(tile_row, tile_col, table, row_blocks, pieces):
    count = tile_row.shape[1]
    tiles = count // pieces
    lanes = table.shape[1]
    across = jnp.broadcast_to(tile_col[...] * row_blocks + tile_row[...], (tiles, count))
    s = lax.broadcasted_iota(jnp.int32, (tiles, count), 0)
    t = lax.broadcasted_iota(jnp.int32, (tiles, count), 1)
    lane = lax.broadcasted_iota(jnp.int32, (tiles, lanes), 1)
    index = lax.broadcasted_iota(jnp.int32, (tiles, lanes), 0)
    for p in range(pieces):
        here = t - p * tiles
        down = jnp.sum(jnp.where(s == here, across, 0), axis=1, keepdims=True)
        before = jnp.logical_or(across < down, jnp.logical_and(across == down, here < s))
        before = jnp.logical_and(before, jnp.logical_and(here >= 0, here < tiles))
        rank = jnp.sum(before.astype(jnp.int32), axis=1, keepdims=True)
        placed = rank == lane
        below = jnp.sum((down <= lane).astype(jnp.int32), axis=0, keepdims=True)
        equal = jnp.sum((down == lane).astype(jnp.int32), axis=0, keepdims=True)
        ordered = jnp.sum(jnp.where(placed, index, 0), axis=0, keepdims=True)
        places = jnp.sum(jnp.where(placed, down, 0), axis=0, keepdims=True)
        table[3 * p : 3 * p + 1, :] = ordered + p * tiles
        table[3 * p + 1 : 3 * p + 2, :] = places
        table[3 * p + 2 : 3 * p + 3, :] = (
            jnp.where(equal > 0, below - 1, tiles) + p * (tiles + 1)
        )


def sum_tiles(tiles, order, sums, p, pieces):
    size = tiles.shape[1]
    count = tiles.shape[0] // pieces
    first = p * (count + 1)
    sums[first + count] = jnp.zeros((size, size), F32)

    def add(r, total):
        again = order[3 * p + 1, r] == order[3 * p + 1, jnp.maximum(r - 1, 0)]
        total = jnp.where(again, total, 0.0) + tiles[order[3 * p, r]].astype(F32)
        sums[first + r] = total
        return total

    lax.fori_loop(0, count, add, jnp.zeros((size, size), F32), unroll=4)


def dense_column(order, sums, high, low, c, pieces):
    size = sums.shape[1]
    row_blocks = high.shape[1] // size
    for k in range(row_blocks):
        value = None
        for p in range(pieces):
            piece = sums[order[3 * p + 2, c * row_blocks + k]]
            value = piece if value is None else value + piece
        rounded = value.astype(BF16)
        high[c, k * size : (k + 1) * size] = rounded
        low[c, k * size : (k + 1) * size] = (value - rounded.astype(F32)).astype(BF16)


def iterate_kernel(
    n, chains, tiles_in, tile_row_in, tile_col_in, primal_in, objective_in, upper_in, dual_in,
    bound_in, primal_end, dual_end,
    tiles, tile_row, tile_col, primal_start, objective, upper, dual_start, row_bound,
    table, order, summed, high, low, far_high, far_low, high_turned, low_turned,
    flipped, bounds, packed, state, dual, bound,
    part_own, part_send, part_recv, own, send1, recv1, spread,
    sl, st, sp, rp, sa, ra, sd, rd, si, ri, s1, r1, sx, rx, se, re,
):
    me = lax.axis_index("row")
    core = lax.rem(me, 2)
    chip = me // 2
    chips = n // 2
    partner = me + 1 - 2 * core
    size = primal_in.shape[0]
    rows = dual_in.shape[0]
    mine = primal_in.shape[1] // 2
    part = mine // chains

    def chip_at(d):
        return lax.bitwise_xor(chip, d)

    def peer(d):
        return chip_at(d) * 2 + core

    def send(src, dst, send_sem, recv_sem, device):
        return pltpu.make_async_remote_copy(
            src_ref=src, dst_ref=dst, send_sem=send_sem, recv_sem=recv_sem,
            device_id={"row": device}, device_id_type=pl.DeviceIdType.MESH,
        )

    def whole(h):
        return pl.ds(h * mine, mine)

    def chain(c):
        return pl.ds(c * part, part)

    def place(c):
        return pl.ds(core * mine + c * part, part)

    def load(k):
        src, dst = (
            (tile_col_in, tile_col), (tile_row_in, tile_row), (dual_in, dual_start),
            (primal_in, primal_start), (objective_in, objective), (upper_in, upper),
            (bound_in, row_bound),
        )[k]
        return pltpu.make_async_copy(src, dst, sl.at[k])

    def load_tiles(p):
        here = pl.ds(p * (tiles.shape[0] // PIECES), tiles.shape[0] // PIECES)
        return pltpu.make_async_copy(tiles_in.at[here], tiles.at[here], st.at[1 + p])

    def first_partial(c, d):
        return send(
            part_send.at[c, d], part_recv.at[c, d], sp.at[c, d], rp.at[c, d], partner
        )

    def matrix(k):
        src, dst = ((high, far_high), (low, far_low))[k]
        return send(src, dst, sa.at[k], ra.at[k], partner)

    def rows_over(k):
        src, dst = ((flipped, dual), (bounds, bound))[k]
        return send(src.at[whole(1 - core)], dst.at[1], sd.at[k], rd.at[k], partner)

    def start_state():
        return send(packed.at[1 - core], state.at[core], si, ri, partner)

    def reduce(c, d):
        return send(send1.at[c, d], recv1.at[c, d], s1.at[c, d], r1.at[c, d], peer(d))

    def gather(c, d):
        return send(spread.at[c, 0], spread.at[c, d], sx.at[c, d], rx.at[c, d], peer(d))

    def primal_back(c):
        return send(
            state.at[1 - core, chain(c)], primal_end.at[place(c)], se.at[0, c], re.at[0, c], partner
        )

    def dual_back(c):
        return send(
            dual.at[1, chain(c)], dual_end.at[place(c)], se.at[1, c], re.at[1, c], partner
        )

    far_first = [*range(chips - 1, 1, -2), *range(chips - 2, 0, -2), 1]
    near_first = list(range(1, chips))
    arrival = [
        d for low, top in ((1, chips // 2), (chips // 2, chips)) for odd in (1, 0)
        for d in range(top - 1, low - 1, -1) if d % 2 == odd
    ]

    def dot(left, right):
        return lax.dot_general(
            left, right, (((1,), (0,)), ((), ())), preferred_element_type=F32
        )

    def columns(left, d, pairs):
        q = 2 * chip_at(d)
        total = None
        for refs in pairs:
            right = jnp.concatenate(
                [jnp.concatenate([ref[q], ref[q + 1]], axis=1) for ref in refs], axis=0
            )
            value = dot(left, right)
            total = value if total is None else total + value
        return [total[:, k * size : (k + 1) * size] for k in range(2)]

    def start():
        left = jnp.concatenate([flipped[whole(core), :], flipped[whole(1 - core), :]], axis=0)
        left = left.astype(BF16)
        for d in far_first + [0]:
            for k in range(2):
                dense_column(order, summed, high, low, 2 * chip_at(d) + k, PIECES)
            for k, piece in enumerate(columns(left, d, ((high,), (low,)))):
                for c in range(chains):
                    at = c * part
                    part_own[c, d, k] = piece[at : at + part]
                    part_send[c, d, k] = piece[mine + at : mine + at + part].astype(BF16)
    def finish_start():
        for c in range(chains):
            for d in far_first + [0]:
                first_partial(c, d).wait_recv()
                value = part_own[c, d] + part_recv[c, d].astype(F32)
                if d:
                    send1[c, d] = value.astype(BF16)
                    reduce(c, d).start()
                else:
                    own[c] = value

    def turn(pairs, at):
        @pl.loop(0, high.shape[0], unroll=4)
        def _(b):
            for source, target in pairs:
                target[b, :, at : at + rows] = source[b].T

    def partials(c):
        left = jnp.concatenate([dual[0, chain(c), :], dual[1, chain(c), :]], axis=1)
        left = left.astype(BF16)
        for d in far_first + [0]:
            for k, piece in enumerate(columns(left, d, ((high, far_high), (low, far_low)))):
                if d:
                    send1[c, d, k] = piece.astype(BF16)
                else:
                    own[c, k] = piece
            if d:
                reduce(c, d).start()

    def update(c):
        total = own[c]
        for d in near_first:
            reduce(c, d).wait_recv()
            total += recv1[c, d].astype(F32)
        before = state[:, chain(c), :]
        cost = state[:, pl.ds(mine + c * part, part), :]
        upper_here = state[:, pl.ds(2 * mine, 1), :]
        updated = jnp.clip(before - STEP * (cost - total), 0.0, upper_here)
        spread[c, 0] = (2.0 * updated - before).astype(BF16)
        for d in far_first:
            gather(c, d).start()
        state[:, chain(c), :] = updated
        for d in near_first:
            reduce(c, d).wait_send()

    def image(c):
        total = None
        for d in [0] + arrival:
            if d:
                gather(c, d).wait_recv()
            q = 2 * chip_at(d)
            left = jnp.concatenate([spread[c, d, k] for k in range(2)], axis=1)
            for ref in (high_turned, low_turned):
                right = jnp.concatenate([ref[q], ref[q + 1]], axis=0)
                value = dot(left, right)
                total = value if total is None else total + value
        for k in range(2):
            dual[k, chain(c), :] = jnp.maximum(
                dual[k, chain(c), :]
                + STEP * (bound[k, chain(c), :] - total[:, k * rows : (k + 1) * rows]),
                0.0,
            )
        for d in near_first:
            gather(c, d).wait_send()

    barrier = pltpu.get_barrier_semaphore()
    others = [partner] + [peer(d) for d in near_first]
    for other in others:
        pl.semaphore_signal(
            barrier, inc=1, device_id={"row": other}, device_id_type=pl.DeviceIdType.MESH
        )
    load(0).start()
    load(1).start()
    for p in range(PIECES):
        load_tiles(p).start()
    load(2).start()
    load(0).wait()
    load(1).wait()
    order_tiles(tile_row, tile_col, table, rows // size, PIECES)
    to_scalars = pltpu.make_async_copy(table, order, st.at[0])
    to_scalars.start()
    to_scalars.wait()
    for p in range(PIECES):
        load_tiles(p).wait()
        sum_tiles(tiles, order, summed, p, PIECES)
    for k in range(3, 7):
        load(k).start()
    load(2).wait()
    flipped[...] = dual_start[...].T
    start()
    pl.semaphore_wait(barrier, len(others))
    for c in range(chains):
        for d in far_first + [0]:
            first_partial(c, d).start()
    finish_start()
    for k in range(3, 7):
        load(k).wait()
    for source, offset in ((primal_start, 0), (objective, mine)):
        value = source[...].T
        for h in range(2):
            packed[h, pl.ds(offset, mine), :] = value[h * mine : (h + 1) * mine]
    for h in range(2):
        packed[h, pl.ds(2 * mine, 8), :] = jnp.broadcast_to(upper[...], (8, size))
    bounds[...] = row_bound[...].T
    start_state().start()
    for k in range(2):
        rows_over(k).start()
    for k in range(2):
        matrix(k).start()
    state[core] = packed[core]
    dual[0] = flipped[whole(core), :]
    bound[0] = bounds[whole(core), :]
    turn(((high, high_turned), (low, low_turned)), 0)
    start_state().wait()

    def finish_matrix():
        for k in range(2):
            rows_over(k).wait()
            matrix(k).wait()
        turn(((far_high, high_turned), (far_low, low_turned)), rows)
        for c in range(chains):
            for d in range(chips):
                first_partial(c, d).wait_send()

    def iteration(step, carry):
        more = step < ITERS - 1
        for c in range(chains):
            update(c)

            @pl.when(jnp.logical_not(more))
            def _():
                primal_back(c).start()

        pl.when(step == 0)(finish_matrix)
        for c in range(chains):
            image(c)
            pl.when(more)(functools.partial(partials, c))

            @pl.when(jnp.logical_not(more))
            def _():
                dual_back(c).start()

        return carry

    lax.fori_loop(0, ITERS, iteration, 0)
    for c in range(chains):
        primal_end[place(c), :] = state[core, chain(c), :]
        dual_end[place(c), :] = dual[0, chain(c), :]
    for c in range(chains):
        primal_back(c).wait()
        dual_back(c).wait()


def body(
    tile_values, tile_row, tile_col, primal_start, objective, upper_bound, dual_start, row_bound
):
    n = lax.axis_size("row")
    size = tile_values.shape[1]
    count = primal_start.shape[1]
    blocks = n * primal_start.shape[0] // size
    chips = n // 2
    assert blocks == n and n % 2 == 0 and chips & (chips - 1) == 0
    rows = dual_start.shape[0]
    row_blocks = rows // size
    tiles = tile_values.shape[0]
    chains = CHAINS
    mine = count // 2
    part = mine // chains
    lanes = -(-max(tiles, blocks * row_blocks) // 128) * 128
    table_rows = -(-3 * PIECES // 8) * 8
    table = pltpu.VMEM((table_rows, lanes), jnp.int32)
    vmem = pl.BlockSpec(memory_space=pltpu.VMEM)
    dma = pltpu.SemaphoreType.DMA
    matrix = pltpu.VMEM((blocks, rows, size), BF16)
    column = pltpu.VMEM(primal_start.shape, F32)
    row = pltpu.VMEM(dual_start.shape, F32)
    row_flipped = pltpu.VMEM((count, rows), F32)
    turned = pltpu.VMEM((blocks, size, 2 * rows), BF16)
    pieces = pltpu.VMEM((chains, chips, 2, part, size), BF16)
    primal_end, dual_end = pl.pallas_call(
        functools.partial(iterate_kernel, n, chains),
        out_shape=(
            pltpu.VMEM((count, size), F32), pltpu.VMEM((count, rows), F32)
        ),
        in_specs=[pl.BlockSpec(memory_space=pltpu.HBM)] * 8,
        out_specs=(vmem, vmem),
        scratch_shapes=[
            pltpu.VMEM(tile_values.shape, BF16),
            pltpu.VMEM((1, tiles), jnp.int32), pltpu.VMEM((1, tiles), jnp.int32),
            column, column, pltpu.VMEM((1, size), F32), row, row,
            table, pltpu.SMEM((table_rows, lanes), jnp.int32),
            pltpu.VMEM((tiles + PIECES, size, size), F32),
            matrix, matrix, matrix, matrix, turned, turned,
            row_flipped, row_flipped,
            pltpu.VMEM((2, count + 8, size), F32), pltpu.VMEM((2, count + 8, size), F32),
            pltpu.VMEM((2, mine, rows), F32), pltpu.VMEM((2, mine, rows), F32),
            pltpu.VMEM((chains, chips, 2, part, size), F32), pieces, pieces,
            pltpu.VMEM((chains, 2, part, size), F32), pieces, pieces, pieces,
            dma((7,)), dma((1 + PIECES,)),
        ]
        + [dma((chains, chips))] * 2 + [dma((2,))] * 4 + [dma(())] * 2
        + [dma((chains, chips))] * 4 + [dma((2, chains))] * 2,
        compiler_params=pltpu.CompilerParams(
            collective_id=0, has_side_effects=True, vmem_limit_bytes=66000000
        ),
    )(
        tile_values, tile_row.reshape(1, -1), tile_col.reshape(1, -1), primal_start, objective,
        upper_bound.reshape(1, -1), dual_start, row_bound,
    )
    return pl.pallas_call(
        finish_kernel,
        out_shape=(
            jax.ShapeDtypeStruct(primal_start.shape, F32),
            jax.ShapeDtypeStruct(dual_start.shape, F32),
        ),
        in_specs=[vmem] * 2,
        out_specs=(vmem, vmem),
        compiler_params=pltpu.CompilerParams(vmem_limit_bytes=1 << 20),
    )(primal_end, dual_end)


def solution(mesh):
    rows = P(("parts", "row"), None)
    flat = P(("parts", "row"))
    return jax.shard_map(
        body,
        mesh=mesh,
        in_specs=(P(("parts", "row"), None, None), flat, flat, rows, rows, flat, rows, rows),
        out_specs=(rows, rows),
        check_vma=False,
    )
```

```python
import functools

import jax
import jax.numpy as jnp
from jax import lax
from jax.experimental import pallas as pl
from jax.experimental.pallas import tpu as pltpu
from jax.sharding import PartitionSpec as P

ITERS = 3
CHAINS = 2
PIECES = 1
STEP = 0.4
F32 = jnp.float32
BF16 = jnp.bfloat16


def finish_kernel(primal, dual, primal_out, dual_out, primal_turned, dual_turned, sems):
    size = primal.shape[1]
    copies = []
    for k in range(dual.shape[1] // size):
        here = pl.ds(k * size, size)
        dual_turned[here, :] = dual[:, here].T
        copies.append(
            pltpu.make_async_copy(dual_turned.at[here], dual_out.at[here], sems.at[k + 1])
        )
        copies[-1].start()
    primal_turned[...] = primal[...].T
    copies.append(pltpu.make_async_copy(primal_turned, primal_out, sems.at[0]))
    copies[-1].start()
    for copy in copies:
        copy.wait()


def order_tiles(tile_row, tile_col, table, row_blocks, pieces):
    count = tile_row.shape[1]
    tiles = count // pieces
    lanes = table.shape[1]
    across = jnp.broadcast_to(tile_col[...] * row_blocks + tile_row[...], (tiles, count))
    s = lax.broadcasted_iota(jnp.int32, (tiles, count), 0)
    t = lax.broadcasted_iota(jnp.int32, (tiles, count), 1)
    lane = lax.broadcasted_iota(jnp.int32, (tiles, lanes), 1)
    index = lax.broadcasted_iota(jnp.int32, (tiles, lanes), 0)
    for p in range(pieces):
        here = t - p * tiles
        down = jnp.sum(jnp.where(s == here, across, 0), axis=1, keepdims=True)
        before = jnp.logical_or(across < down, jnp.logical_and(across == down, here < s))
        before = jnp.logical_and(before, jnp.logical_and(here >= 0, here < tiles))
        rank = jnp.sum(before.astype(jnp.int32), axis=1, keepdims=True)
        placed = rank == lane
        below = jnp.sum((down <= lane).astype(jnp.int32), axis=0, keepdims=True)
        equal = jnp.sum((down == lane).astype(jnp.int32), axis=0, keepdims=True)
        ordered = jnp.sum(jnp.where(placed, index, 0), axis=0, keepdims=True)
        places = jnp.sum(jnp.where(placed, down, 0), axis=0, keepdims=True)
        table[3 * p : 3 * p + 1, :] = ordered + p * tiles
        table[3 * p + 1 : 3 * p + 2, :] = places
        table[3 * p + 2 : 3 * p + 3, :] = (
            jnp.where(equal > 0, below - 1, tiles) + p * (tiles + 1)
        )


def sum_tiles(tiles, order, sums, p, pieces):
    size = tiles.shape[1]
    count = tiles.shape[0] // pieces
    first = p * (count + 1)
    sums[first + count] = jnp.zeros((size, size), F32)

    def add(r, total):
        again = order[3 * p + 1, r] == order[3 * p + 1, jnp.maximum(r - 1, 0)]
        total = jnp.where(again, total, 0.0) + tiles[order[3 * p, r]].astype(F32)
        sums[first + r] = total
        return total

    lax.fori_loop(0, count, add, jnp.zeros((size, size), F32), unroll=4)


def dense_column(order, sums, high, low, c, pieces):
    size = sums.shape[1]
    row_blocks = high.shape[1] // size
    for k in range(row_blocks):
        value = None
        for p in range(pieces):
            piece = sums[order[3 * p + 2, c * row_blocks + k]]
            value = piece if value is None else value + piece
        rounded = value.astype(BF16)
        high[c, k * size : (k + 1) * size] = rounded
        low[c, k * size : (k + 1) * size] = (value - rounded.astype(F32)).astype(BF16)


def iterate_kernel(
    n, chains, tiles_in, tile_row_in, tile_col_in, primal_in, objective_in, upper_in, dual_in,
    bound_in, primal_end, dual_end,
    tiles, tile_row, tile_col, primal_start, objective, upper, dual_start, row_bound,
    table, order, summed, high, low, far_high, far_low, high_turned, low_turned,
    flipped, bounds, packed, state, dual, bound,
    part_own, part_send, part_recv, own, send1, recv1, spread,
    sl, st, sp, rp, sa, ra, sd, rd, si, ri, s1, r1, sx, rx, se, re,
):
    me = lax.axis_index("row")
    core = lax.rem(me, 2)
    chip = me // 2
    chips = n // 2
    partner = me + 1 - 2 * core
    size = primal_in.shape[0]
    rows = dual_in.shape[0]
    mine = primal_in.shape[1] // 2
    part = mine // chains

    def chip_at(d):
        return lax.bitwise_xor(chip, d)

    def peer(d):
        return chip_at(d) * 2 + core

    def send(src, dst, send_sem, recv_sem, device):
        return pltpu.make_async_remote_copy(
            src_ref=src, dst_ref=dst, send_sem=send_sem, recv_sem=recv_sem,
            device_id={"row": device}, device_id_type=pl.DeviceIdType.MESH,
        )

    def whole(h):
        return pl.ds(h * mine, mine)

    def chain(c):
        return pl.ds(c * part, part)

    def place(c):
        return pl.ds(core * mine + c * part, part)

    def load(k):
        src, dst = (
            (tile_col_in, tile_col), (tile_row_in, tile_row), (dual_in, dual_start),
            (primal_in, primal_start), (objective_in, objective), (upper_in, upper),
            (bound_in, row_bound),
        )[k]
        return pltpu.make_async_copy(src, dst, sl.at[k])

    def load_tiles(p):
        here = pl.ds(p * (tiles.shape[0] // PIECES), tiles.shape[0] // PIECES)
        return pltpu.make_async_copy(tiles_in.at[here], tiles.at[here], st.at[1 + p])

    def first_partial(c, d):
        return send(
            part_send.at[c, d], part_recv.at[c, d], sp.at[c, d], rp.at[c, d], partner
        )

    def matrix(k):
        src, dst = ((high, far_high), (low, far_low))[k]
        return send(src, dst, sa.at[k], ra.at[k], partner)

    def rows_over(k):
        src, dst = ((flipped, dual), (bounds, bound))[k]
        return send(src.at[whole(1 - core)], dst.at[1], sd.at[k], rd.at[k], partner)

    def start_state():
        return send(packed.at[1 - core], state.at[core], si, ri, partner)

    def reduce(c, d):
        return send(send1.at[c, d], recv1.at[c, d], s1.at[c, d], r1.at[c, d], peer(d))

    def gather(c, d):
        return send(spread.at[c, 0], spread.at[c, d], sx.at[c, d], rx.at[c, d], peer(d))

    def primal_back(c):
        return send(
            state.at[1 - core, chain(c)], primal_end.at[place(c)], se.at[0, c], re.at[0, c], partner
        )

    def dual_back(c):
        return send(
            dual.at[1, chain(c)], dual_end.at[place(c)], se.at[1, c], re.at[1, c], partner
        )

    far_first = [*range(chips - 1, 1, -2), *range(chips - 2, 0, -2), 1]
    near_first = list(range(1, chips))
    arrival = [
        d for low, top in ((1, chips // 2), (chips // 2, chips)) for odd in (1, 0)
        for d in range(top - 1, low - 1, -1) if d % 2 == odd
    ]

    def dot(left, right):
        return lax.dot_general(
            left, right, (((1,), (0,)), ((), ())), preferred_element_type=F32
        )

    def columns(left, d, pairs):
        q = 2 * chip_at(d)
        total = None
        for refs in pairs:
            right = jnp.concatenate(
                [jnp.concatenate([ref[q], ref[q + 1]], axis=1) for ref in refs], axis=0
            )
            value = dot(left, right)
            total = value if total is None else total + value
        return [total[:, k * size : (k + 1) * size] for k in range(2)]

    def start():
        left = jnp.concatenate([flipped[whole(core), :], flipped[whole(1 - core), :]], axis=0)
        left = left.astype(BF16)
        for d in far_first + [0]:
            for k in range(2):
                dense_column(order, summed, high, low, 2 * chip_at(d) + k, PIECES)
            for k, piece in enumerate(columns(left, d, ((high,), (low,)))):
                for c in range(chains):
                    at = c * part
                    part_own[c, d, k] = piece[at : at + part]
                    part_send[c, d, k] = piece[mine + at : mine + at + part].astype(BF16)
    def finish_start():
        for c in range(chains):
            for d in far_first + [0]:
                first_partial(c, d).wait_recv()
                value = part_own[c, d] + part_recv[c, d].astype(F32)
                if d:
                    send1[c, d] = value.astype(BF16)
                    reduce(c, d).start()
                else:
                    own[c] = value

    def turn(pairs, at):
        @pl.loop(0, high.shape[0], unroll=4)
        def _(b):
            for source, target in pairs:
                target[b, :, at : at + rows] = source[b].T

    def partials(c):
        left = jnp.concatenate([dual[0, chain(c), :], dual[1, chain(c), :]], axis=1)
        left = left.astype(BF16)
        for d in far_first + [0]:
            for k, piece in enumerate(columns(left, d, ((high, far_high), (low, far_low)))):
                if d:
                    send1[c, d, k] = piece.astype(BF16)
                else:
                    own[c, k] = piece
            if d:
                reduce(c, d).start()

    def update(c):
        total = own[c]
        for d in near_first:
            reduce(c, d).wait_recv()
            total += recv1[c, d].astype(F32)
        before = state[:, chain(c), :]
        cost = state[:, pl.ds(mine + c * part, part), :]
        upper_here = state[:, pl.ds(2 * mine, 1), :]
        updated = jnp.clip(before - STEP * (cost - total), 0.0, upper_here)
        spread[c, 0] = (2.0 * updated - before).astype(BF16)
        for d in far_first:
            gather(c, d).start()
        state[:, chain(c), :] = updated
        for d in near_first:
            reduce(c, d).wait_send()

    def image(c):
        total = None
        for d in [0] + arrival:
            if d:
                gather(c, d).wait_recv()
            q = 2 * chip_at(d)
            left = jnp.concatenate([spread[c, d, k] for k in range(2)], axis=1)
            for ref in (high_turned, low_turned):
                right = jnp.concatenate([ref[q], ref[q + 1]], axis=0)
                value = dot(left, right)
                total = value if total is None else total + value
        for k in range(2):
            dual[k, chain(c), :] = jnp.maximum(
                dual[k, chain(c), :]
                + STEP * (bound[k, chain(c), :] - total[:, k * rows : (k + 1) * rows]),
                0.0,
            )
        for d in near_first:
            gather(c, d).wait_send()

    barrier = pltpu.get_barrier_semaphore()
    others = [partner] + [peer(d) for d in near_first]
    for other in others:
        pl.semaphore_signal(
            barrier, inc=1, device_id={"row": other}, device_id_type=pl.DeviceIdType.MESH
        )
    load(0).start()
    load(1).start()
    for p in range(PIECES):
        load_tiles(p).start()
    load(2).start()
    load(0).wait()
    load(1).wait()
    order_tiles(tile_row, tile_col, table, rows // size, PIECES)
    to_scalars = pltpu.make_async_copy(table, order, st.at[0])
    to_scalars.start()
    to_scalars.wait()
    for p in range(PIECES):
        load_tiles(p).wait()
        sum_tiles(tiles, order, summed, p, PIECES)
    for k in range(3, 7):
        load(k).start()
    load(2).wait()
    flipped[...] = dual_start[...].T
    start()
    pl.semaphore_wait(barrier, len(others))
    for c in range(chains):
        for d in far_first + [0]:
            first_partial(c, d).start()
    finish_start()
    for k in range(3, 7):
        load(k).wait()
    for source, offset in ((primal_start, 0), (objective, mine)):
        value = source[...].T
        for h in range(2):
            packed[h, pl.ds(offset, mine), :] = value[h * mine : (h + 1) * mine]
    for h in range(2):
        packed[h, pl.ds(2 * mine, 8), :] = jnp.broadcast_to(upper[...], (8, size))
    bounds[...] = row_bound[...].T
    start_state().start()
    for k in range(2):
        rows_over(k).start()
    for k in range(2):
        matrix(k).start()
    state[core] = packed[core]
    dual[0] = flipped[whole(core), :]
    bound[0] = bounds[whole(core), :]
    turn(((high, high_turned), (low, low_turned)), 0)
    start_state().wait()

    def finish_matrix():
        for k in range(2):
            rows_over(k).wait()
            matrix(k).wait()
        turn(((far_high, high_turned), (far_low, low_turned)), rows)
        for c in range(chains):
            for d in range(chips):
                first_partial(c, d).wait_send()

    def iteration(step):
        more = step < ITERS - 1
        for c in range(chains):
            update(c)
            if not more:
                primal_back(c).start()
        if step == 0:
            finish_matrix()
        for c in range(chains):
            image(c)
            if more:
                partials(c)
            else:
                dual_back(c).start()
    for step in range(ITERS):
        iteration(step)
    for c in range(chains):
        primal_end[place(c), :] = state[core, chain(c), :]
        dual_end[place(c), :] = dual[0, chain(c), :]
    for c in range(chains):
        primal_back(c).wait()
        dual_back(c).wait()


def body(
    tile_values, tile_row, tile_col, primal_start, objective, upper_bound, dual_start, row_bound
):
    n = lax.axis_size("row")
    size = tile_values.shape[1]
    count = primal_start.shape[1]
    blocks = n * primal_start.shape[0] // size
    chips = n // 2
    assert blocks == n and n % 2 == 0 and chips & (chips - 1) == 0
    rows = dual_start.shape[0]
    row_blocks = rows // size
    tiles = tile_values.shape[0]
    chains = CHAINS
    mine = count // 2
    part = mine // chains
    lanes = -(-max(tiles, blocks * row_blocks) // 128) * 128
    table_rows = -(-3 * PIECES // 8) * 8
    table = pltpu.VMEM((table_rows, lanes), jnp.int32)
    vmem = pl.BlockSpec(memory_space=pltpu.VMEM)
    dma = pltpu.SemaphoreType.DMA
    matrix = pltpu.VMEM((blocks, rows, size), BF16)
    column = pltpu.VMEM(primal_start.shape, F32)
    row = pltpu.VMEM(dual_start.shape, F32)
    row_flipped = pltpu.VMEM((count, rows), F32)
    turned = pltpu.VMEM((blocks, size, 2 * rows), BF16)
    pieces = pltpu.VMEM((chains, chips, 2, part, size), BF16)
    primal_end, dual_end = pl.pallas_call(
        functools.partial(iterate_kernel, n, chains),
        out_shape=(
            pltpu.VMEM((count, size), F32), pltpu.VMEM((count, rows), F32)
        ),
        in_specs=[pl.BlockSpec(memory_space=pltpu.HBM)] * 8,
        out_specs=(vmem, vmem),
        scratch_shapes=[
            pltpu.VMEM(tile_values.shape, BF16),
            pltpu.VMEM((1, tiles), jnp.int32), pltpu.VMEM((1, tiles), jnp.int32),
            column, column, pltpu.VMEM((1, size), F32), row, row,
            table, pltpu.SMEM((table_rows, lanes), jnp.int32),
            pltpu.VMEM((tiles + PIECES, size, size), F32),
            matrix, matrix, matrix, matrix, turned, turned,
            row_flipped, row_flipped,
            pltpu.VMEM((2, count + 8, size), F32), pltpu.VMEM((2, count + 8, size), F32),
            pltpu.VMEM((2, mine, rows), F32), pltpu.VMEM((2, mine, rows), F32),
            pltpu.VMEM((chains, chips, 2, part, size), F32), pieces, pieces,
            pltpu.VMEM((chains, 2, part, size), F32), pieces, pieces, pieces,
            dma((7,)), dma((1 + PIECES,)),
        ]
        + [dma((chains, chips))] * 2 + [dma((2,))] * 4 + [dma(())] * 2
        + [dma((chains, chips))] * 4 + [dma((2, chains))] * 2,
        compiler_params=pltpu.CompilerParams(
            collective_id=0, has_side_effects=True, vmem_limit_bytes=66000000
        ),
    )(
        tile_values, tile_row.reshape(1, -1), tile_col.reshape(1, -1), primal_start, objective,
        upper_bound.reshape(1, -1), dual_start, row_bound,
    )
    return pl.pallas_call(
        finish_kernel,
        out_shape=(
            jax.ShapeDtypeStruct(primal_start.shape, F32),
            jax.ShapeDtypeStruct(dual_start.shape, F32),
        ),
        in_specs=[vmem] * 2,
        out_specs=(pl.BlockSpec(memory_space=pltpu.HBM),) * 2,
        scratch_shapes=[column, row, dma((1 + row_blocks,))],
        compiler_params=pltpu.CompilerParams(vmem_limit_bytes=1 << 20),
    )(primal_end, dual_end)


def solution(mesh):
    rows = P(("parts", "row"), None)
    flat = P(("parts", "row"))
    return jax.shard_map(
        body,
        mesh=mesh,
        in_specs=(P(("parts", "row"), None, None), flat, flat, rows, rows, flat, rows, rows),
        out_specs=(rows, rows),
        check_vma=False,
    )
```

```python
import functools

import jax
import jax.numpy as jnp
from jax import lax
from jax.experimental import pallas as pl
from jax.experimental.pallas import tpu as pltpu
from jax.sharding import PartitionSpec as P

ITERS = 3
CHAINS = 2
PIECES = 1
STEP = 0.4
F32 = jnp.float32
BF16 = jnp.bfloat16


def finish_kernel(primal, dual, primal_out, dual_out, primal_turned, dual_turned, sems):
    size = primal.shape[1]
    copies = []
    for k in range(dual.shape[1] // size):
        here = pl.ds(k * size, size)
        dual_turned[here, :] = dual[:, here].T
        copies.append(
            pltpu.make_async_copy(dual_turned.at[here], dual_out.at[here], sems.at[k + 1])
        )
        copies[-1].start()
    primal_turned[...] = primal[...].T
    copies.append(pltpu.make_async_copy(primal_turned, primal_out, sems.at[0]))
    copies[-1].start()
    for copy in copies:
        copy.wait()


def order_tiles(tile_row, tile_col, table, row_blocks, pieces):
    count = tile_row.shape[1]
    tiles = count // pieces
    lanes = table.shape[1]
    across = jnp.broadcast_to(tile_col[...] * row_blocks + tile_row[...], (tiles, count))
    s = lax.broadcasted_iota(jnp.int32, (tiles, count), 0)
    t = lax.broadcasted_iota(jnp.int32, (tiles, count), 1)
    lane = lax.broadcasted_iota(jnp.int32, (tiles, lanes), 1)
    index = lax.broadcasted_iota(jnp.int32, (tiles, lanes), 0)
    for p in range(pieces):
        here = t - p * tiles
        down = jnp.sum(jnp.where(s == here, across, 0), axis=1, keepdims=True)
        before = jnp.logical_or(across < down, jnp.logical_and(across == down, here < s))
        before = jnp.logical_and(before, jnp.logical_and(here >= 0, here < tiles))
        rank = jnp.sum(before.astype(jnp.int32), axis=1, keepdims=True)
        placed = rank == lane
        below = jnp.sum((down <= lane).astype(jnp.int32), axis=0, keepdims=True)
        equal = jnp.sum((down == lane).astype(jnp.int32), axis=0, keepdims=True)
        ordered = jnp.sum(jnp.where(placed, index, 0), axis=0, keepdims=True)
        places = jnp.sum(jnp.where(placed, down, 0), axis=0, keepdims=True)
        table[3 * p : 3 * p + 1, :] = ordered + p * tiles
        table[3 * p + 1 : 3 * p + 2, :] = places
        table[3 * p + 2 : 3 * p + 3, :] = (
            jnp.where(equal > 0, below - 1, tiles) + p * (tiles + 1)
        )


def sum_tiles(tiles, order, sums, p, pieces):
    size = tiles.shape[1]
    count = tiles.shape[0] // pieces
    first = p * (count + 1)
    sums[first + count] = jnp.zeros((size, size), F32)

    def add(r, total):
        again = order[3 * p + 1, r] == order[3 * p + 1, jnp.maximum(r - 1, 0)]
        total = jnp.where(again, total, 0.0) + tiles[order[3 * p, r]].astype(F32)
        sums[first + r] = total
        return total

    lax.fori_loop(0, count, add, jnp.zeros((size, size), F32), unroll=4)


def dense_column(order, sums, high, low, c, pieces):
    size = sums.shape[1]
    row_blocks = high.shape[1] // size
    for k in range(row_blocks):
        value = None
        for p in range(pieces):
            piece = sums[order[3 * p + 2, c * row_blocks + k]]
            value = piece if value is None else value + piece
        rounded = value.astype(BF16)
        high[c, k * size : (k + 1) * size] = rounded
        low[c, k * size : (k + 1) * size] = (value - rounded.astype(F32)).astype(BF16)


def iterate_kernel(
    n, chains, tiles_in, tile_row_in, tile_col_in, primal_in, objective_in, upper_in, dual_in,
    bound_in, primal_end, dual_end,
    tiles, tile_row, tile_col, primal_start, objective, upper, dual_start, row_bound,
    table, order, summed, high, low, far_high, far_low, high_turned, low_turned,
    flipped, bounds, packed, state, dual, bound,
    part_own, part_send, part_recv, own, send1, recv1, spread,
    sl, st, sp, rp, sa, ra, sd, rd, si, ri, s1, r1, sx, rx, se, re,
):
    me = lax.axis_index("row")
    core = lax.rem(me, 2)
    chip = me // 2
    chips = n // 2
    partner = me + 1 - 2 * core
    size = primal_in.shape[0]
    rows = dual_in.shape[0]
    mine = primal_in.shape[1] // 2
    part = mine // chains

    def chip_at(d):
        return lax.bitwise_xor(chip, d)

    def peer(d):
        return chip_at(d) * 2 + core

    def send(src, dst, send_sem, recv_sem, device):
        return pltpu.make_async_remote_copy(
            src_ref=src, dst_ref=dst, send_sem=send_sem, recv_sem=recv_sem,
            device_id={"row": device}, device_id_type=pl.DeviceIdType.MESH,
        )

    def whole(h):
        return pl.ds(h * mine, mine)

    def chain(c):
        return pl.ds(c * part, part)

    def place(c):
        return pl.ds(core * mine + c * part, part)

    def load(k):
        src, dst = (
            (tile_col_in, tile_col), (tile_row_in, tile_row), (dual_in, dual_start),
            (primal_in, primal_start), (objective_in, objective), (upper_in, upper),
            (bound_in, row_bound),
        )[k]
        return pltpu.make_async_copy(src, dst, sl.at[k])

    def load_tiles(p):
        here = pl.ds(p * (tiles.shape[0] // PIECES), tiles.shape[0] // PIECES)
        return pltpu.make_async_copy(tiles_in.at[here], tiles.at[here], st.at[1 + p])

    def first_partial(c, d):
        return send(
            part_send.at[c, d], part_recv.at[c, d], sp.at[c, d], rp.at[c, d], partner
        )

    def matrix(k):
        src, dst = ((high, far_high), (low, far_low))[k]
        return send(src, dst, sa.at[k], ra.at[k], partner)

    def rows_over(k):
        src, dst = ((flipped, dual), (bounds, bound))[k]
        return send(src.at[whole(1 - core)], dst.at[1], sd.at[k], rd.at[k], partner)

    def start_state():
        return send(packed.at[1 - core], state.at[core], si, ri, partner)

    def reduce(c, d):
        return send(send1.at[c, d], recv1.at[c, d], s1.at[c, d], r1.at[c, d], peer(d))

    def gather(c, d):
        return send(spread.at[c, 0], spread.at[c, d], sx.at[c, d], rx.at[c, d], peer(d))

    def primal_back(c):
        return send(
            state.at[1 - core, chain(c)], primal_end.at[place(c)], se.at[0, c], re.at[0, c], partner
        )

    def dual_back(c):
        return send(
            dual.at[1, chain(c)], dual_end.at[place(c)], se.at[1, c], re.at[1, c], partner
        )

    far_first = [*range(chips - 1, 1, -2), *range(chips - 2, 0, -2), 1]
    near_first = list(range(1, chips))
    arrival = [
        d for low, top in ((1, chips // 2), (chips // 2, chips)) for odd in (1, 0)
        for d in range(top - 1, low - 1, -1) if d % 2 == odd
    ]

    def dot(left, right):
        return lax.dot_general(
            left, right, (((1,), (0,)), ((), ())), preferred_element_type=F32
        )

    def columns(left, d, pairs):
        q = 2 * chip_at(d)
        total = None
        for refs in pairs:
            right = jnp.concatenate(
                [jnp.concatenate([ref[q], ref[q + 1]], axis=1) for ref in refs], axis=0
            )
            value = dot(left, right)
            total = value if total is None else total + value
        return [total[:, k * size : (k + 1) * size] for k in range(2)]

    def start():
        left = jnp.concatenate([flipped[whole(core), :], flipped[whole(1 - core), :]], axis=0)
        left = left.astype(BF16)
        for d in far_first + [0]:
            for k in range(2):
                dense_column(order, summed, high, low, 2 * chip_at(d) + k, PIECES)
            for k, piece in enumerate(columns(left, d, ((high,), (low,)))):
                for c in range(chains):
                    at = c * part
                    part_own[c, d, k] = piece[at : at + part]
                    part_send[c, d, k] = piece[mine + at : mine + at + part].astype(BF16)
    def finish_start():
        for c in range(chains):
            for d in far_first + [0]:
                first_partial(c, d).wait_recv()
                value = part_own[c, d] + part_recv[c, d].astype(F32)
                if d:
                    send1[c, d] = value.astype(BF16)
                    reduce(c, d).start()
                else:
                    own[c] = value

    def turn(pairs, at):
        @pl.loop(0, high.shape[0], unroll=8)
        def _(b):
            for source, target in pairs:
                target[b, :, at : at + rows] = source[b].T

    def partials(c):
        left = jnp.concatenate([dual[0, chain(c), :], dual[1, chain(c), :]], axis=1)
        left = left.astype(BF16)
        for d in far_first + [0]:
            for k, piece in enumerate(columns(left, d, ((high, far_high), (low, far_low)))):
                if d:
                    send1[c, d, k] = piece.astype(BF16)
                else:
                    own[c, k] = piece
            if d:
                reduce(c, d).start()

    def update(c, more):
        total = own[c]
        for d in near_first:
            reduce(c, d).wait_recv()
            total += recv1[c, d].astype(F32)
        before = state[:, chain(c), :]
        cost = state[:, pl.ds(mine + c * part, part), :]
        upper_here = state[:, pl.ds(2 * mine, 1), :]
        updated = jnp.clip(before - STEP * (cost - total), 0.0, upper_here)
        spread[c, 0] = (2.0 * updated - before).astype(BF16)
        if more:
            for d in far_first:
                gather(c, d).start()
        else:
            for q in range(chips):
                pl.when(chip != q)(gather(c, lax.bitwise_xor(chip, q)).start)
        state[:, chain(c), :] = updated

    def image(c):
        total = None
        for d in [0] + arrival:
            if d:
                gather(c, d).wait_recv()
            q = 2 * chip_at(d)
            left = jnp.concatenate([spread[c, d, k] for k in range(2)], axis=1)
            for ref in (high_turned, low_turned):
                right = jnp.concatenate([ref[q], ref[q + 1]], axis=0)
                value = dot(left, right)
                total = value if total is None else total + value
        for k in range(2):
            dual[k, chain(c), :] = jnp.maximum(
                dual[k, chain(c), :]
                + STEP * (bound[k, chain(c), :] - total[:, k * rows : (k + 1) * rows]),
                0.0,
            )
        for d in near_first:
            reduce(c, d).wait_send()
            gather(c, d).wait_send()

    barrier = pltpu.get_barrier_semaphore()
    others = [partner] + [peer(d) for d in near_first]
    for other in others:
        pl.semaphore_signal(
            barrier, inc=1, device_id={"row": other}, device_id_type=pl.DeviceIdType.MESH
        )
    load(0).start()
    load(1).start()
    for p in range(PIECES):
        load_tiles(p).start()
    load(2).start()
    load(0).wait()
    load(1).wait()
    order_tiles(tile_row, tile_col, table, rows // size, PIECES)
    to_scalars = pltpu.make_async_copy(table, order, st.at[0])
    to_scalars.start()
    to_scalars.wait()
    for p in range(PIECES):
        load_tiles(p).wait()
        sum_tiles(tiles, order, summed, p, PIECES)
    for k in range(3, 7):
        load(k).start()
    load(2).wait()
    flipped[...] = dual_start[...].T
    start()
    pl.semaphore_wait(barrier, len(others))
    for c in range(chains):
        for d in far_first + [0]:
            first_partial(c, d).start()
    finish_start()
    for k in range(3, 7):
        load(k).wait()
    for source, offset in ((primal_start, 0), (objective, mine)):
        value = source[...].T
        for h in range(2):
            packed[h, pl.ds(offset, mine), :] = value[h * mine : (h + 1) * mine]
    for h in range(2):
        packed[h, pl.ds(2 * mine, 8), :] = jnp.broadcast_to(upper[...], (8, size))
    bounds[...] = row_bound[...].T
    start_state().start()
    for k in range(2):
        rows_over(k).start()
    for k in range(2):
        matrix(k).start()
    state[core] = packed[core]
    dual[0] = flipped[whole(core), :]
    bound[0] = bounds[whole(core), :]
    turn(((high, high_turned), (low, low_turned)), 0)
    start_state().wait()

    def finish_matrix():
        for k in range(2):
            rows_over(k).wait()
            matrix(k).wait()
        turn(((far_high, high_turned), (far_low, low_turned)), rows)
        for c in range(chains):
            for d in range(chips):
                first_partial(c, d).wait_send()

    def iteration(step):
        more = step < ITERS - 1
        for c in range(chains):
            update(c, more)
            if not more:
                primal_back(c).start()
        if step == 0:
            finish_matrix()
        for c in range(chains):
            image(c)
            if more:
                partials(c)
            else:
                dual_back(c).start()
    for step in range(ITERS):
        iteration(step)
    for c in range(chains):
        primal_end[place(c), :] = state[core, chain(c), :]
        dual_end[place(c), :] = dual[0, chain(c), :]
    for c in range(chains):
        primal_back(c).wait()
        dual_back(c).wait()


def body(
    tile_values, tile_row, tile_col, primal_start, objective, upper_bound, dual_start, row_bound
):
    n = lax.axis_size("row")
    size = tile_values.shape[1]
    count = primal_start.shape[1]
    blocks = n * primal_start.shape[0] // size
    chips = n // 2
    assert blocks == n and n % 2 == 0 and chips & (chips - 1) == 0
    rows = dual_start.shape[0]
    row_blocks = rows // size
    tiles = tile_values.shape[0]
    chains = CHAINS
    mine = count // 2
    part = mine // chains
    lanes = -(-max(tiles, blocks * row_blocks) // 128) * 128
    table_rows = -(-3 * PIECES // 8) * 8
    table = pltpu.VMEM((table_rows, lanes), jnp.int32)
    vmem = pl.BlockSpec(memory_space=pltpu.VMEM)
    dma = pltpu.SemaphoreType.DMA
    matrix = pltpu.VMEM((blocks, rows, size), BF16)
    column = pltpu.VMEM(primal_start.shape, F32)
    row = pltpu.VMEM(dual_start.shape, F32)
    row_flipped = pltpu.VMEM((count, rows), F32)
    turned = pltpu.VMEM((blocks, size, 2 * rows), BF16)
    pieces = pltpu.VMEM((chains, chips, 2, part, size), BF16)
    primal_end, dual_end = pl.pallas_call(
        functools.partial(iterate_kernel, n, chains),
        out_shape=(
            pltpu.VMEM((count, size), F32), pltpu.VMEM((count, rows), F32)
        ),
        in_specs=[pl.BlockSpec(memory_space=pltpu.HBM)] * 8,
        out_specs=(vmem, vmem),
        scratch_shapes=[
            pltpu.VMEM(tile_values.shape, BF16),
            pltpu.VMEM((1, tiles), jnp.int32), pltpu.VMEM((1, tiles), jnp.int32),
            column, column, pltpu.VMEM((1, size), F32), row, row,
            table, pltpu.SMEM((table_rows, lanes), jnp.int32),
            pltpu.VMEM((tiles + PIECES, size, size), F32),
            matrix, matrix, matrix, matrix, turned, turned,
            row_flipped, row_flipped,
            pltpu.VMEM((2, count + 8, size), F32), pltpu.VMEM((2, count + 8, size), F32),
            pltpu.VMEM((2, mine, rows), F32), pltpu.VMEM((2, mine, rows), F32),
            pltpu.VMEM((chains, chips, 2, part, size), F32), pieces, pieces,
            pltpu.VMEM((chains, 2, part, size), F32), pieces, pieces, pieces,
            dma((7,)), dma((1 + PIECES,)),
        ]
        + [dma((chains, chips))] * 2 + [dma((2,))] * 4 + [dma(())] * 2
        + [dma((chains, chips))] * 4 + [dma((2, chains))] * 2,
        compiler_params=pltpu.CompilerParams(
            collective_id=0, has_side_effects=True, vmem_limit_bytes=66000000
        ),
    )(
        tile_values, tile_row.reshape(1, -1), tile_col.reshape(1, -1), primal_start, objective,
        upper_bound.reshape(1, -1), dual_start, row_bound,
    )
    return pl.pallas_call(
        finish_kernel,
        out_shape=(
            jax.ShapeDtypeStruct(primal_start.shape, F32),
            jax.ShapeDtypeStruct(dual_start.shape, F32),
        ),
        in_specs=[vmem] * 2,
        out_specs=(pl.BlockSpec(memory_space=pltpu.HBM),) * 2,
        scratch_shapes=[column, row, dma((1 + row_blocks,))],
        compiler_params=pltpu.CompilerParams(vmem_limit_bytes=1 << 20),
    )(primal_end, dual_end)


def solution(mesh):
    rows = P(("parts", "row"), None)
    flat = P(("parts", "row"))
    return jax.shard_map(
        body,
        mesh=mesh,
        in_specs=(P(("parts", "row"), None, None), flat, flat, rows, rows, flat, rows, rows),
        out_specs=(rows, rows),
        check_vma=False,
    )
```
